32 devices in a mesh: expert: 4 (over x, core), tensor: 4 (over z), kv: 2 (over y).
Axes of the slice: x: 2, y: 2, z: 4, core: 2. Of those that a mesh axis runs over, the one named last changes fastest.
Arguments:
- residual_stream: bfloat16 [1024, 4096], P('expert', ('tensor', 'kv')), may hold values from -13 to 13
- grad_output: bfloat16 [1024, 4096], P('expert', ('tensor', 'kv')), may hold values from -6 to 6
- norm_gain: bfloat16 [4096], P(('tensor', 'kv')), may hold values from 0.5 to 1.5
- expert_ids: int32 [1024, 2], P('expert'), may hold values from 0 to 3, all different within a row; in each aligned block of 256 rows (0 to 255, 256 to 511, ...) at most 160 rows name the same one
- gate_probs: float32 [1024, 2], P('expert'), may hold values from 0.1 to 0.9
- w_gate: bfloat16 [4, 14336, 4096], P('expert', ('tensor', 'kv')), may hold values from -0.125 to 0.125
- w_up: bfloat16 [4, 14336, 4096], P('expert', ('tensor', 'kv')), may hold values from -0.125 to 0.125
- w_down: bfloat16 [4, 14336, 4096], P('expert', ('tensor', 'kv')), may hold values from -0.046875 to 0.046875
Outputs:
- input_grad: bfloat16 [1024, 4096], P('expert', ('tensor', 'kv'))
The draws below stay inside these ranges and needn't reach their ends.
Inputs may be any that keep to these rules, and one draw needn't show every extreme that they name: `expert_ids`: each row names two different experts. In each aligned block of 256 rows (the rows of one index of the expert axis) no expert is named by more than 160 rows, a bound that some block reaches.
All inputs are finite; a program needn't handle non-finite values.
Results may differ from the reference program's by a relative error of at most 0.018.
Values may be sent and summed in bfloat16 or wider, within the bound.
A program may use at most 128 MiB of HBM per device.

```python
import math
import jax
import jax.numpy as jnp
import numpy as np
from jax import lax

D = 4096
FF = 14336
TOK_DEV = 256
CAP = 160
EXPERTS = 4
TOKENS = 1024
N_EXPERT = 4


def draw_residual_stream(key, part):
    keys = jax.random.split(jax.random.fold_in(key, 17), 3)
    row_scale = 10.0 ** jax.random.uniform(keys[0], (TOKENS, 1), jnp.float32, -1.5, -0.5)
    ramp = jnp.arange(D, dtype=jnp.float32)[None, :] / D
    col_scale = 10.0 ** (0.5 * ramp + 0.5 * jax.random.uniform(keys[1], (1, D), jnp.float32))
    base = jax.random.normal(keys[2], (TOKENS, D), jnp.float32)
    base = jnp.clip(base, -4.0, 4.0)
    return (base * row_scale * col_scale).astype(jnp.bfloat16)


def with_spikes(drawn, own_key, source, target, blocks, factor):
    owner, partner = [(jnp.arange(drawn.shape[dim]) // (drawn.shape[dim] // blocks)).reshape([-1 if axis == dim else 1 for axis in range(drawn.ndim)]) for dim in (source, target)]
    chosen = jax.random.permutation(own_key, blocks)[partner]
    strong = (owner == chosen) | (owner == (partner + blocks // 2) % blocks)
    return jnp.where(strong, factor * drawn, drawn)


def shard_levels(own_key, dims, cuts, low, top_value):
    factor_of, own = 1.0, jax.random.fold_in(own_key, 6)
    for axis_at, blocks in cuts:
        heights = jnp.exp(jax.random.uniform(jax.random.fold_in(own, axis_at), (blocks,), jnp.float32, low / len(cuts), top_value / len(cuts)))
        factor_of = factor_of * jnp.repeat(heights, dims[axis_at] // blocks).reshape([-1 if axis == axis_at else 1 for axis in range(len(dims))])
    return factor_of


def routed_block(stream_key, own, number, rows, amount, top, bound, skew):
    order = jax.random.permutation(stream_key, amount)
    packed, usual = portions_of(amount, rows * top, bound, skew, True), portions_of(amount, rows * top, bound, skew, False)
    places = jnp.arange(amount)

    def named(tallies, rotation):
        used = int((tallies > 0).sum())
        fixed = max(1, used // 4)
        moved = fixed + (places - fixed + rotation * (used - fixed)) % max(1, amount - fixed)
        return jnp.zeros((amount,), jnp.int32).at[order[jnp.where(places < fixed, places, moved)]].set(jnp.asarray(tallies, jnp.int32))

    tallies = jnp.where(number % 4 == 0, named(packed, number // 4), named(usual, number - number // 4 - 1))
    mixed = jax.random.permutation(jax.random.fold_in(own, 3), amount)
    donor, taker = mixed[0:amount // 2 * 2:2], mixed[1:amount // 2 * 2:2]
    slack = jnp.minimum(tallies[donor] - 1, bound - tallies[taker]) // 2
    slack = jnp.where((donor == order[0]) | (taker == order[0]) | (tallies[taker] == 0), 0, jnp.maximum(slack, 0))
    moved = jax.random.randint(jax.random.fold_in(own, 4), (amount // 2,), 0, 1 << 20) % (slack + 1)
    tallies = tallies.at[donor].add(-moved).at[taker].add(moved)
    items = jnp.searchsorted(jnp.cumsum(tallies), jnp.arange(rows * top), side="right").astype(jnp.int32)
    table = items.reshape(top, rows).T
    table = table[jax.random.permutation(jax.random.fold_in(own, 1), rows)]
    rotation = jax.random.randint(jax.random.fold_in(own, 2), (rows, 1), 0, top)
    return jnp.take_along_axis(table, (jnp.arange(top)[None, :] + rotation) % top, axis=1)


def portions_of(amount, total, bound, lean, full):
    loads = [(1 << 20) // math.isqrt(standing ** lean) + 1 for standing in range(1, amount + 1)]
    largest = bound if full else min(bound, max(-(-total // amount), total * loads[0] // sum(loads)))
    least = 1 if total - largest >= amount - 1 else 0
    counts, rest = [largest] + [least] * (amount - 1), total - largest - least * (amount - 1)
    while rest > 0:
        movable = [i for i in range(1, amount) if counts[i] < largest] or [i for i in range(1, amount) if counts[i] < bound]
        whole, remaining = sum([loads[i] for i in movable]), rest
        for i in movable:
            addition = min(bound - counts[i], max(1, remaining * loads[i] // whole), rest)
            counts[i] = counts[i] + addition
            rest = rest - addition
    return np.array(counts)


def centred(own_key, dims, width, limit, cuts=(), kind=jnp.bfloat16):
    factor_of = shard_levels(own_key, dims, cuts, -0.22, 0.18) if cuts else 1.0
    drawn = jax.random.normal(own_key, dims, jnp.float32) * width * factor_of
    return jnp.minimum(jnp.maximum(drawn, -limit), limit).astype(kind)


def bell_draw_with(stream_key, shape, scale, most, cuts, heavy, kind=jnp.bfloat16):
    values = scale * jax.random.normal(stream_key, shape, jnp.float32)
    if cuts:
        values = values * shard_levels(stream_key, shape, cuts, -0.22, 0.18)
    return jnp.clip(with_spikes(values, jax.random.fold_in(stream_key, 3), *heavy), -most, most).astype(kind)


def setup_inputs(seed: int = 0) -> dict:
    seeds = jax.random.split(jax.random.key(seed), 9)
    residual_stream = draw_residual_stream(jax.random.fold_in(seeds[8], 71), 0)
    grad_output = centred(seeds[1], (TOKENS, D), 1.0, 6.0, ((0, 4), (1, 8)))
    norm_gain = jnp.clip(1.0 + 0.1 * jax.random.normal(seeds[2], (D,), jnp.float32), 0.5, 1.5).astype(jnp.bfloat16)
    expert_ids_keys = jax.random.split(jax.random.fold_in(seeds[3], 1), TOKENS // TOK_DEV)
    expert_ids_turns = jax.random.permutation(jax.random.fold_in(seeds[3], 3), TOKENS // TOK_DEV)
    expert_ids = jax.vmap(lambda own, number: routed_block(jax.random.fold_in(seeds[3], 2), own, number, TOK_DEV, EXPERTS, 2, CAP, 2))(expert_ids_keys, expert_ids_turns).reshape((TOKENS, 2))
    gate_probs = jnp.clip(0.1 + 0.79999997 * jax.random.uniform(seeds[4], (TOKENS, 2), jnp.float32) ** shard_levels(seeds[4], (TOKENS, 2), ((0, 4),), -0.2, 0.2), 0.1, 0.9)
    w_gate = bell_draw_with(seeds[5], (EXPERTS, FF, D), D ** -0.5, 0.125, ((0, 4), (1, 8)), (1, 2, 8, 2.0))
    w_up = bell_draw_with(seeds[6], (EXPERTS, FF, D), D ** -0.5, 0.125, ((0, 4), (1, 8)), (1, 2, 8, 2.0))
    w_down = centred(seeds[7], (EXPERTS, FF, D), FF ** -0.5, 0.046875, ((0, 4), (1, 8)))
    return dict(residual_stream=residual_stream, grad_output=grad_output, norm_gain=norm_gain, expert_ids=expert_ids, gate_probs=gate_probs, w_gate=w_gate, w_up=w_up, w_down=w_down)


epsilon = 1e-05
contract_width = (((1,), (1,)), ((), ()))

def slot_matrix(ids_block, experts):
    flattened = ids_block.reshape(-1)
    onehot = (flattened[:, None] == jnp.arange(experts, dtype=jnp.int32)[None, :]).astype(jnp.int32)
    before = jnp.cumsum(onehot, axis=0) - onehot
    position = lax.optimization_barrier(jnp.sum(before * onehot, axis=1))
    slot_index = flattened * CAP + position
    table = jnp.arange(experts * CAP, dtype=jnp.int32)
    return (slot_index[None, :] == table[:, None]).astype(jnp.bfloat16)

def dispatch_block(ids_block, normed_block, grad_block, prob_block):
    table = slot_matrix(ids_block, EXPERTS)
    repeated_x = jnp.repeat(normed_block, 2, axis=0)
    scaled = (jnp.repeat(grad_block.astype(jnp.float32), 2, axis=0) * prob_block.reshape(-1, 1)).astype(jnp.bfloat16)
    routed_x = jnp.dot(table, repeated_x, preferred_element_type=jnp.float32).astype(jnp.bfloat16)
    routed_grad = jnp.dot(table, scaled, preferred_element_type=jnp.float32).astype(jnp.bfloat16)
    return (table, routed_x, routed_grad)

def expert_grad(operands):
    routed_x, routed_grad, gate_weight, up_weight, down_weight = operands
    gate_value = lax.dot_general(routed_x, gate_weight, contract_width, preferred_element_type=jnp.float32)
    up_value = lax.dot_general(routed_x, up_weight, contract_width, preferred_element_type=jnp.float32)
    act_grad = lax.dot_general(routed_grad, down_weight, contract_width, preferred_element_type=jnp.float32)
    sigmoid_gate = jax.nn.sigmoid(gate_value)
    activated = gate_value * sigmoid_gate
    gate_grad = (act_grad * up_value * sigmoid_gate * (1.0 + gate_value * (1.0 - sigmoid_gate))).astype(jnp.bfloat16)
    up_grad = (act_grad * activated).astype(jnp.bfloat16)
    slot_grad = jnp.dot(gate_grad, gate_weight, preferred_element_type=jnp.float32)
    slot_grad = slot_grad + jnp.dot(up_grad, up_weight, preferred_element_type=jnp.float32)
    return slot_grad.astype(jnp.bfloat16)

def combine_block(table, values):
    summed = lax.dot_general(table, values, (((0,), (0,)), ((), ())), preferred_element_type=jnp.float32)
    return summed.reshape(TOK_DEV, 2, D).sum(axis=1)

def reference(residual_stream, grad_output, norm_gain, expert_ids, gate_probs, w_gate, w_up, w_down):
    stream = residual_stream.astype(jnp.float32)
    squares = lax.optimization_barrier(jnp.sum(stream * stream, axis=1, keepdims=True))
    inverse_rms = lax.rsqrt(squares / D + epsilon)
    gains = norm_gain.astype(jnp.float32)
    normed = (stream * inverse_rms * gains).astype(jnp.bfloat16)
    blocks = N_EXPERT
    tables, routed_x, routed_grad = jax.vmap(dispatch_block)(expert_ids.reshape(blocks, TOK_DEV, 2), normed.reshape(blocks, TOK_DEV, D), grad_output.reshape(blocks, TOK_DEV, D), gate_probs.reshape(blocks, TOK_DEV, 2))
    expert_x = routed_x.reshape(blocks, EXPERTS, CAP, D).transpose(1, 0, 2, 3).reshape(EXPERTS, blocks * CAP, D)
    expert_dy = routed_grad.reshape(blocks, EXPERTS, CAP, D).transpose(1, 0, 2, 3).reshape(EXPERTS, blocks * CAP, D)
    expert_out = lax.map(expert_grad, (expert_x, expert_dy, w_gate, w_up, w_down))
    returned = expert_out.reshape(EXPERTS, blocks, CAP, D).transpose(1, 0, 2, 3).reshape(blocks, EXPERTS * CAP, D)
    token_grad = jax.vmap(combine_block)(tables, returned).reshape(TOKENS, D)
    scaled_grad = token_grad * gains
    projection = lax.optimization_barrier(jnp.sum(scaled_grad * stream, axis=1, keepdims=True))
    result = inverse_rms * scaled_grad - stream * inverse_rms ** 3 * projection / D
    return result.astype(jnp.bfloat16)
```

```python
import functools

import jax
import jax.numpy as jnp
from jax import lax
from jax.experimental import pallas as pl
from jax.experimental.pallas import tpu as pltpu
from jax.sharding import PartitionSpec as P

D = 4096
CAP = 160


epsilon = 1e-05
contract_width = (((1,), (1,)), ((), ()))
contract_hidden = (((0,), (1,)), ((), ()))
contract_slots = (((0,), (0,)), ((), ()))


def slot_matrix(ids_block, experts):
    flattened = ids_block.reshape(-1)
    onehot = (flattened[:, None] == jnp.arange(experts, dtype=jnp.int32)[None, :]).astype(jnp.int32)
    before = jnp.cumsum(onehot, axis=0) - onehot
    position = jnp.sum(before * onehot, axis=1)
    slot_index = flattened * CAP + position
    table = jnp.arange(experts * CAP, dtype=jnp.int32)
    return (slot_index[None, :] == table[:, None]).astype(jnp.bfloat16)


def shards(residual_stream, grad_output, norm_gain, expert_ids, gate_probs, w_gate, w_up, w_down):
    experts = lax.axis_size("expert")
    local_width = residual_stream.shape[1]
    tokens_here = residual_stream.shape[0]
    stream = residual_stream.astype(jnp.float32)
    squares = lax.psum(jnp.sum(stream * stream, axis=1), ("tensor", "kv"))
    inverse_rms = lax.rsqrt(squares / D + epsilon)[:, None]
    gains = norm_gain.astype(jnp.float32)
    normed = (stream * inverse_rms * gains).astype(jnp.bfloat16)
    table = slot_matrix(expert_ids, experts)
    repeated_x = jnp.repeat(normed, 2, axis=0)
    scaled = (
        jnp.repeat(grad_output.astype(jnp.float32), 2, axis=0) * gate_probs.reshape(-1, 1)
    ).astype(jnp.bfloat16)
    routed_x = jnp.dot(table, repeated_x, preferred_element_type=jnp.float32).astype(jnp.bfloat16)
    routed_grad = jnp.dot(table, scaled, preferred_element_type=jnp.float32).astype(jnp.bfloat16)
    routed_x = routed_x.reshape(experts, CAP, local_width)
    routed_grad = routed_grad.reshape(experts, CAP, local_width)
    gate_weight, up_weight, down_weight = (w_gate[0], w_up[0], w_down[0])
    pieces_x = lax.all_to_all(routed_x, "expert", split_axis=0, concat_axis=0, tiled=True)
    pieces_dy = lax.all_to_all(routed_grad, "expert", split_axis=0, concat_axis=0, tiled=True)
    full_x = lax.all_gather(pieces_x, ("tensor", "kv"), axis=2, tiled=True)
    full_dy = lax.all_gather(pieces_dy, ("tensor", "kv"), axis=2, tiled=True)
    leading = full_x.shape[0]
    items = full_x.shape[1]
    matrix_x = full_x.reshape(leading * items, D)
    matrix_dy = full_dy.reshape(leading * items, D)
    gate_value = lax.dot_general(
        matrix_x, gate_weight, contract_width, preferred_element_type=jnp.float32
    )
    up_value = lax.dot_general(
        matrix_x, up_weight, contract_width, preferred_element_type=jnp.float32
    )
    act_grad = lax.dot_general(
        matrix_dy, down_weight, contract_width, preferred_element_type=jnp.float32
    )
    sigmoid_gate = jax.nn.sigmoid(gate_value)
    activated = gate_value * sigmoid_gate
    gate_grad = (
        act_grad * up_value * sigmoid_gate * (1.0 + gate_value * (1.0 - sigmoid_gate))
    ).astype(jnp.bfloat16)
    up_grad = (act_grad * activated).astype(jnp.bfloat16)
    total = lax.dot_general(
        gate_weight, gate_grad, contract_hidden, preferred_element_type=jnp.float32
    )
    summed = lax.psum_scatter(
        total
        + lax.dot_general(up_weight, up_grad, contract_hidden, preferred_element_type=jnp.float32),
        ("tensor", "kv"),
        scatter_dimension=0,
        tiled=True,
    )
    returned = summed.T.astype(jnp.bfloat16).reshape(leading, items, local_width)
    combined = lax.all_to_all(returned, "expert", split_axis=0, concat_axis=0, tiled=True)
    gathered = lax.dot_general(
        table,
        combined.reshape(experts * CAP, local_width),
        contract_slots,
        preferred_element_type=jnp.float32,
    )
    token_grad = gathered.reshape(tokens_here, 2, local_width).sum(axis=1)
    scaled_grad = token_grad * gains
    projection = lax.psum(jnp.sum(scaled_grad * stream, axis=1), ("tensor", "kv"))[:, None]
    result = inverse_rms * scaled_grad - stream * inverse_rms**3 * projection / D
    return result.astype(jnp.bfloat16)


MESH = pl.DeviceIdType.MESH
TILE = 256
T = 4
BLOCKS = 2 * T
ORDER = [
    "1a0", "0f1", "1a1", "0g0", "0f0", "2a0", "C000", "D00", "1g0", "3a0", "C100", "C010", "0g1", "1g1", "0h0",
    "3a1", "D10", "0h1", "C001", "2g0", "D01", "2a1", "e1", "3g0", "2f0", "C101", "e0", "C030", "e2", "3f0",
    "3f1", "D30", "C020", "2f1", "e3", "3g1", "D20", "1x1", "C120", "1x0", "C130", "2h0", "2g1", "3h1", "C110",
    "C021", "3h0", "2h1", "D21", "1x2", "C031", "D31", "1x3", "C131", "C111", "C121", "C011", "D11",
]

EXTRA = [(1, 0, 1), (0, 1, 0), (0, 1, 1), (1, 1, 1)]
RETURN = [(d, s) for d in (1, 2, 3, 0) for s in (1, 0)]


def atoms_of(order):
    atoms, ahead = [], []
    for token in order:
        if token[0] == "C":
            atoms.append(dict(a=int(token[1]), i=int(token[2]), s=int(token[3]), ahead=ahead, middle=[]))
            ahead = []
        elif token[0] == "D":
            atoms[-1]["middle"], ahead = ahead, []
        else:
            ahead.append(token)
    return atoms, ahead


def pick(index, values):
    result = jnp.int32(values[0])
    for k, value in enumerate(values[1:], 1):
        if value != values[k - 1]:
            result = jnp.where(index >= k, value, result)
    return result


def fused_kernel(
    x_ref, dy_ref, gain_ref, ids_ref, prob_ref, wg_ref, wu_ref, wd_ref, out_ref,
    tok, acc, wab, wb, hid, routed, crecv, xrecv, yrecv, zrecv, gains, metas, sel, prob,
    ssq, own_sq, psend, precv, own_x, own_gain, own_meta,
    ag_send, ag_recv, line_send, line_recv, extra_send, extra_recv, rs_send, rs_recv,
    small_send, small_recv, wasem, wbsem, lsem,
):
    e = lax.axis_index("expert")
    z = lax.axis_index("tensor")
    y = lax.axis_index("kv")
    core = e + 1 - 2 * lax.rem(e, 2)
    across = lax.rem(e + 2, 4)
    partner = z + 1 - 2 * lax.rem(z, 2)
    tokens, width = out_ref.shape
    half = tokens // 2
    hidden = wg_ref.shape[0]
    tiles = hidden // TILE
    inputs = (x_ref, dy_ref)
    low = z < 2
    layer = [z, partner, jnp.where(low, 2, 1), jnp.where(low, 3, 0)]

    def z_of(d):
        return lax.rem(z + T - d, T)

    def y_of(s):
        return y if s == 0 else 1 - y

    def fb_of(d, s):
        return z_of(d) * 2 + y_of(s)

    def seen(i, s):
        return layer[i] * 2 + y_of(s)

    def b_of(u, c):
        base = core if c else e
        return lax.rem(base + 2 * u, 4)

    def remote(src, dst, send, recv, peer):
        return pltpu.make_async_remote_copy(
            src_ref=src, dst_ref=dst, send_sem=send, recv_sem=recv,
            device_id=peer, device_id_type=MESH,
        )

    def slot(a, i, s, u, c=0):
        return tok.at[a, seen(i, s), b_of(u, c)]

    def number(a, i, s, u, c):
        return (((a * T + i) * 2 + s) * 2 + u) * 2 + c

    across_peer, side_peer, core_peer = (across, z, y), (e, z, 1 - y), (core, z, y)

    def source(a, i, s, u):
        return inputs[a] if (i, s, u) == (0, 0, 0) else slot(a, i, s, u)

    def gather_copy(a, i, s, u, c=0):
        n = number(a, i, s, u, c)
        if c:
            src, there, peer = (s, u), slot(a, i, s, u), core_peer
        elif (u and not s) or (s and u and a == 0):
            src, peer = (s, 0), across_peer
            there = slot(a, i, s, 0)
        else:
            src, peer = (0, u), side_peer
            there = slot(a, i, 0, u)
        return remote(source(a, i, *src), there, ag_send.at[n], ag_recv.at[n], peer)

    def gather_wait(a, i, s, u, c=0):
        n = number(a, i, s, u, c)
        here = slot(a, i, s, u, c)
        remote(here, here, ag_send.at[n], ag_recv.at[n], core_peer).wait_recv()

    def extra_copy(k):
        a, s, u = EXTRA[k]
        here = slot(a, 0, s, u)
        return remote(here, here, extra_send.at[k], extra_recv.at[k], (e, partner, y))

    def extra_wait(k):
        a, s, u = EXTRA[k]
        here = slot(a, 1, s, u)
        remote(here, here, extra_send.at[k], extra_recv.at[k], (e, partner, y)).wait_recv()

    def own_line(a, way):
        return remote(
            inputs[a], tok.at[a, fb_of(0, 0), e], line_send.at[a, way], line_recv.at[a, z],
            (e, z + 2 * way - 1, y),
        )

    def pass_on(a, i):
        v = layer[i]
        here = slot(a, i, 0, 0)
        return remote(
            here, here, line_send.at[a, 1 + i], line_recv.at[a, v],
            (e, jnp.where(v < z, z + 1, z - 1), y),
        )

    def passes(i):
        return jnp.where(layer[i] < z, z < T - 1, z > 0)

    sent = []

    def send(*item):
        sent.append(item)
        gather_copy(*item).start()

    def full(i):
        return i != 1

    def event(token):
        if token[0] == "e":
            extra_copy(int(token[1])).start()
            return
        i, kind, k = int(token[0]), token[1], int(token[2])
        if kind == "a":
            pass_on(k, i).wait_recv()

            @pl.when(passes(i))
            def _():
                pass_on(k, i).start()

            if full(i):
                send(k, i, *((1, 0) if k == 0 else (0, 1)))
                send(k, i, *((0, 1) if k == 0 else (1, 0)))
            else:
                send(k, i, *((0, 1) if k == 0 else (1, 0)))
            send(k, i, 0, 0, 1)
            return
        if kind == "x":
            extra_wait(k)
            send(EXTRA[k][0], i, *EXTRA[k][1:], 1)
            return
        first = (1, 0) if k == 0 else (0, 1)
        s, u = {"f": first, "g": first[::-1], "h": (1, 1)}[kind]
        gather_wait(k, i, s, u)
        if kind == "f":
            send(k, i, 1, 1)
        send(k, i, s, u, 1)

    atoms, rest = atoms_of(ORDER)
    wide = [atom for atom in atoms if atom["a"] == 0]
    tall = [atom for atom in atoms if atom["a"] == 1]

    def fb_at(index, group):
        return select(index, [layer[atom["i"]] * 2 + y_of(atom["s"]) for atom in group])

    def select(index, values):
        result = values[0]
        for k, value in enumerate(values[1:], 1):
            result = jnp.where(index >= k, value, result)
        return result

    return_fb = [fb_of(*item) for item in RETURN]

    def columns_of(fb):
        return pl.ds(pl.multiple_of(fb * width, width), width)

    def wide_copies(index, place):
        columns = columns_of(place)
        at = lax.rem(index, 2)
        return [
            pltpu.make_async_copy(ref.at[:, columns], wab.at[at, k], wasem.at[at, k])
            for k, ref in enumerate((wg_ref, wu_ref))
        ]

    def tall_copy(index, place):
        at = lax.rem(index, 2)
        return pltpu.make_async_copy(wd_ref.at[:, columns_of(place)], wb.at[at], wbsem.at[at])

    local = [
        pltpu.make_async_copy(x_ref, tok.at[0, fb_of(0, 0), e], lsem.at[0]),
        pltpu.make_async_copy(dy_ref, tok.at[1, fb_of(0, 0), e], lsem.at[1]),
    ]
    peers = [(e, lax.rem(z + d, T), y_of(s)) for d in range(T) for s in (0, 1) if d or s]
    sources = [fb_of(d, s) for d in range(T) for s in (0, 1) if d or s]
    others = [(lax.rem(e + k, 4), z, y) for k in (1, 2, 3)]
    barrier = pltpu.get_barrier_semaphore()
    for peer in peers + others:
        pl.semaphore_signal(barrier, inc=1, device_id=peer, device_id_type=MESH)
    for copy in local:
        copy.start()
    pl.semaphore_wait(barrier, len(peers) + len(others))

    for a in (0, 1):
        for way in (0, 1):
            @pl.when(z < T - 1 if way else z > 0)
            def _():
                own_line(a, way).start()
    for item in ((0, 0, 1, 0), (1, 0, 0, 1), (0, 0, 0, 1), (1, 0, 1, 0), (0, 0, 0, 0, 1), (1, 0, 0, 0, 1)):
        send(*item)
    for copy in wide_copies(0, fb_at(0, wide)) + [tall_copy(0, fb_at(0, tall))]:
        copy.start()

    number_of = lax.broadcasted_iota(jnp.int32, (8, tokens), 0)
    named_by = jnp.where(number_of < 4, number_of, number_of - 4)
    first = jnp.broadcast_to(ids_ref[0:1, :], (8, tokens)) == named_by
    second = jnp.broadcast_to(ids_ref[1:2, :], (8, tokens)) == named_by
    named = jnp.where(first, 1.0, 0.0) + jnp.where(second, 1.0, 0.0)
    later = (
        lax.broadcasted_iota(jnp.int32, (tokens, tokens), 0)
        < lax.broadcasted_iota(jnp.int32, (tokens, tokens), 1)
    )
    before = jnp.dot(
        named.astype(jnp.bfloat16), jnp.where(later, 1.0, 0.0).astype(jnp.bfloat16),
        preferred_element_type=jnp.float32,
    )
    weight = jnp.where(first, jnp.broadcast_to(prob_ref[0:1, :], (8, tokens)), 0.0) + jnp.where(
        second, jnp.broadcast_to(prob_ref[1:2, :], (8, tokens)), 0.0
    )
    own_meta[...] = jnp.where(number_of < 4, jnp.where(named > 0.0, before, -1.0), weight)
    metas[e] = own_meta[...]
    own_gain[...] = jnp.broadcast_to(gain_ref[...].astype(jnp.float32)[None, :], own_gain.shape)
    gains[fb_of(0, 0)] = own_gain[...]

    small = []
    for k, peer in enumerate(others):
        copy = remote(own_meta, metas.at[e], small_send.at[k], small_recv.at[k], peer)
        copy.start()
        there = metas.at[lax.rem(e + 3 - k, 4)]
        small.append((copy, remote(there, there, small_send.at[k], small_recv.at[k], peer)))
    for k, peer in enumerate(peers):
        n = 3 + k
        copy = remote(own_gain, gains.at[fb_of(0, 0)], small_send.at[n], small_recv.at[n], peer)
        copy.start()
        there = gains.at[sources[k]]
        small.append((copy, remote(there, there, small_send.at[n], small_recv.at[n], peer)))

    own_sq[...] = jnp.zeros_like(own_sq)
    ssq[...] = jnp.zeros_like(ssq)

    def clear(n, carry):
        for k in range(3):
            acc[k, n] = jnp.zeros(acc.shape[2:], jnp.float32)
        return carry

    lax.fori_loop(0, tiles, clear, 0)
    for copy, arrival in small[:3]:
        arrival.wait_recv()
    for b in range(4):
        slots = metas[b, pl.ds(e, 1), :]
        probs = metas[b, pl.ds(4 + e, 1), :]
        index = lax.broadcasted_iota(jnp.int32, (CAP, slots.shape[1]), 0).astype(jnp.float32)
        chosen = jnp.where(index == slots, 1.0, 0.0)
        sel[b] = chosen.astype(jnp.bfloat16)
        prob[pl.ds(b * CAP, CAP), :] = jnp.sum(chosen * probs, axis=1, keepdims=True)
    for copy, arrival in small[3:]:
        arrival.wait_recv()
    for copy in local:
        copy.wait()

    def accumulate(k, source, weights):
        for n in range(tiles):
            acc[k, n] += lax.dot_general(
                source[...], weights[n * TILE : (n + 1) * TILE, :], contract_width,
                preferred_element_type=jnp.float32,
            )

    def gather_step(j, carry):
        for k, atom in enumerate(atoms):
            @pl.when(j == k)
            def _():
                for token in atom["ahead"]:
                    event(token)
                for u in (0, 1):
                    gather_wait(atom["a"], atom["i"], atom["s"], u, 1)

        kinds = [atom["a"] for atom in atoms]
        ranks = [sum(kinds[:k]) for k in range(len(atoms))]
        kind = pick(j, kinds)
        tall_rank = pick(j, ranks)
        wide_rank = j - tall_rank

        @pl.when(kind == 0)
        def _():
            following = jnp.where(
                wide_rank < BLOCKS - 1, fb_at(wide_rank + 1, wide), return_fb[0]
            )
            for copy in wide_copies(wide_rank + 1, following):
                copy.start()
            fb = fb_at(wide_rank, wide)
            gain_row = gains[fb, 0:1, :]
            mine = tok[0, fb, e].astype(jnp.float32)
            own_sq[...] += jnp.sum(mine * mine, axis=1, keepdims=True)
            for b in range(4):
                rows = pl.ds(b * CAP, CAP)
                picked = jnp.dot(sel[b], tok[0, fb, b], preferred_element_type=jnp.float32)
                ssq[rows, :] += jnp.sum(picked * picked, axis=1, keepdims=True)
                routed[0, rows, :] = (picked * gain_row).astype(jnp.bfloat16)
            for copy in wide_copies(wide_rank, fb):
                copy.wait()
            at = lax.rem(wide_rank, 2)
            accumulate(0, routed.at[0], wab.at[at, 0])
            for k, atom in enumerate(atoms):
                if atom["middle"]:
                    @pl.when(j == k)
                    def _():
                        for token in atom["middle"]:
                            event(token)
            accumulate(1, routed.at[0], wab.at[at, 1])

        @pl.when(kind == 1)
        def _():
            @pl.when(tall_rank < BLOCKS - 1)
            def _():
                tall_copy(tall_rank + 1, fb_at(tall_rank + 1, tall)).start()

            fb = fb_at(tall_rank, tall)
            for b in range(4):
                rows = pl.ds(b * CAP, CAP)
                picked = jnp.dot(sel[b], tok[1, fb, b], preferred_element_type=jnp.float32)
                routed[1, rows, :] = (picked * prob[rows, :]).astype(jnp.bfloat16)
            tall_copy(tall_rank, fb).wait()
            accumulate(2, routed.at[1], wb.at[lax.rem(tall_rank, 2)])

        return carry

    lax.fori_loop(0, len(atoms), gather_step, 0)
    for token in rest:
        event(token)
    reload = pltpu.make_async_copy(x_ref, own_x, lsem.at[2])
    reload.start()
    for item in sent:
        gather_copy(*item).wait_send()
    for a in (0, 1):
        for way in (0, 1):
            @pl.when(z < T - 1 if way else z > 0)
            def _():
                own_line(a, way).wait_send()
        for i in range(1, T):
            @pl.when(passes(i))
            def _():
                pass_on(a, i).wait_send()
    for k in range(len(EXTRA)):
        extra_copy(k).wait_send()
    for copy, arrival in small:
        copy.wait_send()

    inverse = lax.rsqrt(ssq[...] / D + epsilon)

    def activate(n, carry):
        columns = pl.ds(pl.multiple_of(n * TILE, TILE), TILE)
        gate_value = acc[0, n] * inverse
        up_value = acc[1, n] * inverse
        act_grad = acc[2, n]
        sigmoid_gate = jax.nn.sigmoid(gate_value)
        hid[0, :, columns] = (
            act_grad * up_value * sigmoid_gate * (1.0 + gate_value * (1.0 - sigmoid_gate))
        ).astype(jnp.bfloat16)
        hid[1, :, columns] = (act_grad * gate_value * sigmoid_gate).astype(jnp.bfloat16)
        return carry

    lax.fori_loop(0, tiles, activate, 0)

    upper, lower = pl.ds(0, half), pl.ds(half, half)

    def core_copy(i, u):
        return remote(
            tok.at[0, i, lax.rem(core + 2 * u, 4)], crecv.at[i, u],
            rs_send.at[i, u], rs_recv.at[i, u], core_peer,
        )

    def across_copy(i, h):
        rows = lower if h else upper
        return remote(
            tok.at[1, i, 0, rows], xrecv.at[i, rows], rs_send.at[i, 2 + h], rs_recv.at[i, 2 + h], across_peer
        )

    def side_copy(i, u, h):
        d = RETURN[i][0]
        rows = lower if h else upper
        n = 4 + (u if h else 2)
        return remote(
            tok.at[1, i, 0 if u else 1, rows], yrecv.at[d, u, rows], rs_send.at[i, n], rs_recv.at[i, n], side_peer
        )

    def line_copy(i):
        d = RETURN[i][0]
        return remote(
            tok.at[1, i, 2], zrecv.at[d - 1], rs_send.at[i, 7], rs_recv.at[i, 7], (e, z_of(d), y)
        )

    def total(rows, *parts):
        value = parts[0][rows].astype(jnp.float32)
        for part in parts[1:]:
            value = value + part[rows].astype(jnp.float32)
        return value

    everything = pl.ds(0, tokens)

    def first_stage(i):
        core_copy(i, 1).wait_recv()
        far = (tok.at[0, i, across], crecv.at[i, 1])
        if RETURN[i][1]:
            tok[1, i, 0] = total(everything, *far).astype(jnp.bfloat16)
            across_copy(i, 0).start()
            side_copy(i, 1, 1).start()
            core_copy(i, 0).wait_recv()
            tok[1, i, 1, lower] = total(lower, tok.at[0, i, e], crecv.at[i, 0]).astype(jnp.bfloat16)
            side_copy(i, 0, 1).start()
        else:
            tok[1, i, 0, upper] = total(upper, *far).astype(jnp.bfloat16)
            across_copy(i, 0).start()

    def second_stage(i):
        d, s = RETURN[i]
        if s:
            across_copy(i, 0).wait_recv()
            tok[1, i, 1, upper] = total(
                upper, tok.at[0, i, e], crecv.at[i, 0], xrecv.at[i]
            ).astype(jnp.bfloat16)
            side_copy(i, 0, 0).start()
        else:
            side_copy(i - 1, 1, 1).wait_recv()
            tok[1, i, 0, lower] = total(
                lower, tok.at[0, i, across], crecv.at[i, 1], yrecv.at[d, 1]
            ).astype(jnp.bfloat16)
            across_copy(i, 1).start()

    def third_stage(i):
        d = RETURN[i][0]
        core_copy(i, 0).wait_recv()
        across_copy(i, 0).wait_recv()
        side_copy(i - 1, 0, 1).wait_recv()
        side_copy(i - 1, 0, 0).wait_recv()
        across_copy(i, 1).wait_recv()
        value = total(everything, tok.at[0, i, e], crecv.at[i, 0], xrecv.at[i], yrecv.at[d, 0])
        if d:
            tok[1, i, 2] = value.astype(jnp.bfloat16)
            line_copy(i).start()
        return value

    halves = width // TILE
    stages = {}
    for i, (d, s) in enumerate(RETURN):
        base = halves * (i + 1)
        plan = [(1, first_stage), (4, second_stage)] if s else [(1, first_stage), (2, second_stage), (5, third_stage)]
        for when, stage in plan:
            stages.setdefault(base + when, []).append((stage, i))

    def produce(h, carry):
        for k in range(halves * BLOCKS):
            if k in stages:
                @pl.when(h == k)
                def _():
                    for stage, i in stages[k]:
                        stage(i)

        i, n = h // halves, lax.rem(h, halves)

        @pl.when(jnp.logical_and(n == 0, i < BLOCKS - 1))
        def _():
            for copy in wide_copies(i + 1, select(i + 1, return_fb)):
                copy.start()

        @pl.when(n == 0)
        def _():
            for copy in wide_copies(i, select(i, return_fb)):
                copy.wait()

        at = lax.rem(i, 2)
        columns = pl.ds(pl.multiple_of(n * TILE, TILE), TILE)
        rounded = (
            jnp.dot(hid[0], wab[at, 0, :, columns], preferred_element_type=jnp.float32)
            + jnp.dot(hid[1], wab[at, 1, :, columns], preferred_element_type=jnp.float32)
        ).astype(jnp.bfloat16)
        for b in range(4):
            tok[0, i, b, :, columns] = lax.dot_general(
                sel[b], rounded[b * CAP : (b + 1) * CAP], contract_slots,
                preferred_element_type=jnp.float32,
            ).astype(jnp.bfloat16)

        @pl.when(n == halves - 1)
        def _():
            core_copy(i, 1).start()
            core_copy(i, 0).start()

        return carry

    lax.fori_loop(0, halves * BLOCKS, produce, 0)
    value = None
    for key in sorted(stages):
        if key >= halves * BLOCKS:
            for stage, i in stages[key]:
                value = stage(i)
    reload.wait()
    for i in range(BLOCKS):
        if RETURN[i][1] == 0 and RETURN[i][0]:
            line_copy(i).wait_recv()
            value = value + zrecv[RETURN[i][0] - 1].astype(jnp.float32)

    gain_row = gains[fb_of(0, 0), 0:1, :]
    stream = own_x[...].astype(jnp.float32)
    scaled = value * gain_row
    share = jnp.sum(scaled * stream, axis=1, keepdims=True)
    psend[...] = jnp.broadcast_to(share, (tokens, 128)).T[0:8, :]
    final = []
    for k, peer in enumerate(peers):
        n = 3 + len(peers) + k
        copy = remote(psend, precv.at[k], small_send.at[n], small_recv.at[n], peer)
        copy.start()
        final.append(copy)
    inverse = lax.rsqrt(own_sq[...] / D + epsilon)
    row = psend[...]
    for k, copy in enumerate(final):
        copy.wait_recv()
        row = row + precv[k]
    projection = jnp.broadcast_to(row[0:1, :], (128, tokens)).T[:, 0:1]
    out_ref[...] = (
        inverse * scaled - stream * (inverse * inverse * inverse * projection / D)
    ).astype(out_ref.dtype)
    for copy in final:
        copy.wait_send()
    for i, (d, s) in enumerate(RETURN):
        core_copy(i, 0).wait_send()
        core_copy(i, 1).wait_send()
        across_copy(i, 0).wait_send()
        if s:
            side_copy(i, 1, 1).wait_send()
            side_copy(i, 0, 1).wait_send()
            side_copy(i, 0, 0).wait_send()
        else:
            across_copy(i, 1).wait_send()
            if d:
                line_copy(i).wait_send()


def fused_shards(residual_stream, grad_output, norm_gain, expert_ids, gate_probs, w_gate, w_up, w_down):
    experts = lax.axis_size("expert")
    tokens, width = residual_stream.shape
    hidden = w_gate.shape[1]
    bf16, f32 = jnp.bfloat16, jnp.float32
    rows = experts * CAP
    vmem = pl.BlockSpec(memory_space=pltpu.VMEM)
    hbm = pl.BlockSpec(memory_space=pl.ANY)
    dma = pltpu.SemaphoreType.DMA
    unit = (tokens, width)
    smalls = 3 + 2 * (BLOCKS - 1)
    return pl.pallas_call(
        fused_kernel,
        out_shape=jax.ShapeDtypeStruct(unit, bf16),
        in_specs=[hbm] * 2 + [vmem] * 3 + [hbm] * 3,
        out_specs=vmem,
        scratch_shapes=[
            pltpu.VMEM((2, BLOCKS, experts) + unit, bf16),
            pltpu.VMEM((3, hidden // TILE, rows, TILE), f32),
            pltpu.VMEM((2, 2, hidden, width), bf16),
            pltpu.VMEM((2, hidden, width), bf16),
            pltpu.VMEM((2, rows, hidden), bf16),
            pltpu.VMEM((2, rows, width), bf16),
            pltpu.VMEM((BLOCKS, 2) + unit, bf16),
            pltpu.VMEM((BLOCKS,) + unit, bf16),
            pltpu.VMEM((T, 2) + unit, bf16),
            pltpu.VMEM((T - 1,) + unit, bf16),
            pltpu.VMEM((BLOCKS, 8, width), f32),
            pltpu.VMEM((experts, 8, tokens), f32),
            pltpu.VMEM((experts, CAP, tokens), bf16),
            pltpu.VMEM((rows, 1), f32),
            pltpu.VMEM((rows, 1), f32),
            pltpu.VMEM((tokens, 1), f32),
            pltpu.VMEM((8, tokens), f32),
            pltpu.VMEM((BLOCKS - 1, 8, tokens), f32),
            pltpu.VMEM(unit, bf16),
            pltpu.VMEM((8, width), f32),
            pltpu.VMEM((8, tokens), f32),
            dma((16 * T,)),
            dma((16 * T,)),
            dma((2, T + 1)),
            dma((2, T)),
            dma((len(EXTRA),)),
            dma((len(EXTRA),)),
            dma((BLOCKS, 8)),
            dma((BLOCKS, 8)),
            dma((smalls,)),
            dma((smalls,)),
            dma((2, 2)),
            dma((2,)),
            dma((3,)),
        ],
        compiler_params=pltpu.CompilerParams(
            collective_id=0, has_side_effects=True, vmem_limit_bytes=66000000
        ),
        name="fused",
    )(
        residual_stream, grad_output, norm_gain, expert_ids.T, gate_probs.T,
        w_gate[0], w_up[0], w_down[0],
    )


def solution(mesh):
    placed = (
        P("expert", ("tensor", "kv")),
        P("expert", ("tensor", "kv")),
        P(("tensor", "kv")),
        P("expert", None),
        P("expert", None),
        P("expert", ("tensor", "kv"), None),
        P("expert", ("tensor", "kv"), None),
        P("expert", ("tensor", "kv"), None),
    )
    sizes = dict(mesh.shape)
    width = D // (sizes["tensor"] * sizes["kv"])
    body = fused_shards if sizes == {"expert": 4, "tensor": 4, "kv": 2} and width % 256 == 0 else shards
    return jax.shard_map(
        body, mesh=mesh, in_specs=placed, out_specs=P("expert", ("tensor", "kv")), check_vma=False
    )
```

```python
import functools

import jax
import jax.numpy as jnp
from jax import lax
from jax.experimental import pallas as pl
from jax.experimental.pallas import tpu as pltpu
from jax.sharding import PartitionSpec as P

D = 4096
CAP = 160


epsilon = 1e-05
contract_width = (((1,), (1,)), ((), ()))
contract_hidden = (((0,), (1,)), ((), ()))
contract_slots = (((0,), (0,)), ((), ()))


def slot_matrix(ids_block, experts):
    flattened = ids_block.reshape(-1)
    onehot = (flattened[:, None] == jnp.arange(experts, dtype=jnp.int32)[None, :]).astype(jnp.int32)
    before = jnp.cumsum(onehot, axis=0) - onehot
    position = jnp.sum(before * onehot, axis=1)
    slot_index = flattened * CAP + position
    table = jnp.arange(experts * CAP, dtype=jnp.int32)
    return (slot_index[None, :] == table[:, None]).astype(jnp.bfloat16)


def shards(residual_stream, grad_output, norm_gain, expert_ids, gate_probs, w_gate, w_up, w_down):
    experts = lax.axis_size("expert")
    local_width = residual_stream.shape[1]
    tokens_here = residual_stream.shape[0]
    stream = residual_stream.astype(jnp.float32)
    squares = lax.psum(jnp.sum(stream * stream, axis=1), ("tensor", "kv"))
    inverse_rms = lax.rsqrt(squares / D + epsilon)[:, None]
    gains = norm_gain.astype(jnp.float32)
    normed = (stream * inverse_rms * gains).astype(jnp.bfloat16)
    table = slot_matrix(expert_ids, experts)
    repeated_x = jnp.repeat(normed, 2, axis=0)
    scaled = (
        jnp.repeat(grad_output.astype(jnp.float32), 2, axis=0) * gate_probs.reshape(-1, 1)
    ).astype(jnp.bfloat16)
    routed_x = jnp.dot(table, repeated_x, preferred_element_type=jnp.float32).astype(jnp.bfloat16)
    routed_grad = jnp.dot(table, scaled, preferred_element_type=jnp.float32).astype(jnp.bfloat16)
    routed_x = routed_x.reshape(experts, CAP, local_width)
    routed_grad = routed_grad.reshape(experts, CAP, local_width)
    gate_weight, up_weight, down_weight = (w_gate[0], w_up[0], w_down[0])
    pieces_x = lax.all_to_all(routed_x, "expert", split_axis=0, concat_axis=0, tiled=True)
    pieces_dy = lax.all_to_all(routed_grad, "expert", split_axis=0, concat_axis=0, tiled=True)
    full_x = lax.all_gather(pieces_x, ("tensor", "kv"), axis=2, tiled=True)
    full_dy = lax.all_gather(pieces_dy, ("tensor", "kv"), axis=2, tiled=True)
    leading = full_x.shape[0]
    items = full_x.shape[1]
    matrix_x = full_x.reshape(leading * items, D)
    matrix_dy = full_dy.reshape(leading * items, D)
    gate_value = lax.dot_general(
        matrix_x, gate_weight, contract_width, preferred_element_type=jnp.float32
    )
    up_value = lax.dot_general(
        matrix_x, up_weight, contract_width, preferred_element_type=jnp.float32
    )
    act_grad = lax.dot_general(
        matrix_dy, down_weight, contract_width, preferred_element_type=jnp.float32
    )
    sigmoid_gate = jax.nn.sigmoid(gate_value)
    activated = gate_value * sigmoid_gate
    gate_grad = (
        act_grad * up_value * sigmoid_gate * (1.0 + gate_value * (1.0 - sigmoid_gate))
    ).astype(jnp.bfloat16)
    up_grad = (act_grad * activated).astype(jnp.bfloat16)
    total = lax.dot_general(
        gate_weight, gate_grad, contract_hidden, preferred_element_type=jnp.float32
    )
    summed = lax.psum_scatter(
        total
        + lax.dot_general(up_weight, up_grad, contract_hidden, preferred_element_type=jnp.float32),
        ("tensor", "kv"),
        scatter_dimension=0,
        tiled=True,
    )
    returned = summed.T.astype(jnp.bfloat16).reshape(leading, items, local_width)
    combined = lax.all_to_all(returned, "expert", split_axis=0, concat_axis=0, tiled=True)
    gathered = lax.dot_general(
        table,
        combined.reshape(experts * CAP, local_width),
        contract_slots,
        preferred_element_type=jnp.float32,
    )
    token_grad = gathered.reshape(tokens_here, 2, local_width).sum(axis=1)
    scaled_grad = token_grad * gains
    projection = lax.psum(jnp.sum(scaled_grad * stream, axis=1), ("tensor", "kv"))[:, None]
    result = inverse_rms * scaled_grad - stream * inverse_rms**3 * projection / D
    return result.astype(jnp.bfloat16)


MESH = pl.DeviceIdType.MESH
TILE = 256
T = 4
BLOCKS = 2 * T
ORDER = [
    "0f0", "1a0", "0f1", "2a0", "1a1", "0g0", "2a1", "C000", "0h0", "D00", "C100", "0g1", "0h1", "3a0", "C001",
    "D01", "1g0", "3a1", "2g0", "e2", "e0", "C010", "2f0", "2f1", "D10", "C020", "D20", "C120", "3g0", "1x2",
    "C101", "3f0", "e1", "1g1", "C030", "3f1", "1x0", "2g1", "D30", "C130", "e3", "2h0", "C110", "1x1", "C021",
    "2h1", "D21", "C011", "3h0", "D11", "C121", "3h1", "3g1", "1x3", "C031", "D31", "C111", "C131",
]

EXTRA = [(1, 0, 1), (0, 1, 0), (0, 1, 1), (1, 1, 1)]
RETURN = [(d, s) for d in (1, 2, 3, 0) for s in (1, 0)]


def atoms_of(order):
    atoms, ahead = [], []
    for token in order:
        if token[0] == "C":
            atoms.append(dict(a=int(token[1]), i=int(token[2]), s=int(token[3]), ahead=ahead, middle=[]))
            ahead = []
        elif token[0] == "D":
            atoms[-1]["middle"], ahead = ahead, []
        else:
            ahead.append(token)
    return atoms, ahead


def pick(index, values):
    result = jnp.int32(values[0])
    for k, value in enumerate(values[1:], 1):
        if value != values[k - 1]:
            result = jnp.where(index >= k, value, result)
    return result


def fused_kernel(
    x_ref, dy_ref, gain_hbm, ids_hbm, prob_hbm, wg_ref, wu_ref, wd_ref, out_ref,
    tok, acc, wab, wb, hid, routed, crecv, xrecv, yrecv, zrecv, gains, metas, sel, prob,
    ssq, own_sq, psend, precv, ptotal, pothers, factor, own_x, own_gain, own_meta, gain_ref, ids_ref, prob_ref,
    ag_send, ag_recv, line_send, line_recv, extra_send, extra_recv, rs_send, rs_recv,
    small_send, small_recv, wasem, wbsem, lsem,
):
    e = lax.axis_index("expert")
    z = lax.axis_index("tensor")
    y = lax.axis_index("kv")
    core = e + 1 - 2 * lax.rem(e, 2)
    across = lax.rem(e + 2, 4)
    partner = z + 1 - 2 * lax.rem(z, 2)
    tokens, width = out_ref.shape
    half = tokens // 2
    hidden = wg_ref.shape[0]
    tiles = hidden // TILE
    inputs = (x_ref, dy_ref)
    low = z < 2
    layer = [z, partner, jnp.where(low, 2, 1), jnp.where(low, 3, 0)]

    def z_of(d):
        return lax.rem(z + T - d, T)

    def y_of(s):
        return y if s == 0 else 1 - y

    def fb_of(d, s):
        return z_of(d) * 2 + y_of(s)

    def seen(i, s):
        return layer[i] * 2 + y_of(s)

    def b_of(u, c):
        base = core if c else e
        return lax.rem(base + 2 * u, 4)

    def remote(src, dst, send, recv, peer):
        return pltpu.make_async_remote_copy(
            src_ref=src, dst_ref=dst, send_sem=send, recv_sem=recv,
            device_id=peer, device_id_type=MESH,
        )

    def slot(a, i, s, u, c=0):
        return tok.at[a, seen(i, s), b_of(u, c)]

    def number(a, i, s, u, c):
        return (((a * T + i) * 2 + s) * 2 + u) * 2 + c

    across_peer, side_peer, core_peer = (across, z, y), (e, z, 1 - y), (core, z, y)

    def source(a, i, s, u):
        return inputs[a] if (i, s, u) == (0, 0, 0) else slot(a, i, s, u)

    def gather_copy(a, i, s, u, c=0):
        n = number(a, i, s, u, c)
        if c:
            src, there, peer = (s, u), slot(a, i, s, u), core_peer
        elif (u and not s) or (s and u and a == 0):
            src, peer = (s, 0), across_peer
            there = slot(a, i, s, 0)
        else:
            src, peer = (0, u), side_peer
            there = slot(a, i, 0, u)
        return remote(source(a, i, *src), there, ag_send.at[n], ag_recv.at[n], peer)

    def gather_wait(a, i, s, u, c=0):
        n = number(a, i, s, u, c)
        here = slot(a, i, s, u, c)
        remote(here, here, ag_send.at[n], ag_recv.at[n], core_peer).wait_recv()

    def extra_copy(k):
        a, s, u = EXTRA[k]
        here = slot(a, 0, s, u)
        return remote(here, here, extra_send.at[k], extra_recv.at[k], (e, partner, y))

    def extra_wait(k):
        a, s, u = EXTRA[k]
        here = slot(a, 1, s, u)
        remote(here, here, extra_send.at[k], extra_recv.at[k], (e, partner, y)).wait_recv()

    def own_line(a, way):
        return remote(
            inputs[a], tok.at[a, fb_of(0, 0), e], line_send.at[a, way], line_recv.at[a, z],
            (e, z + 2 * way - 1, y),
        )

    def pass_on(a, i):
        v = layer[i]
        here = slot(a, i, 0, 0)
        return remote(
            here, here, line_send.at[a, 1 + i], line_recv.at[a, v],
            (e, jnp.where(v < z, z + 1, z - 1), y),
        )

    def passes(i):
        return jnp.where(layer[i] < z, z < T - 1, z > 0)

    sent = []

    def send(*item):
        sent.append(item)
        gather_copy(*item).start()

    def full(i):
        return i != 1

    def event(token):
        if token[0] == "e":
            extra_copy(int(token[1])).start()
            return
        i, kind, k = int(token[0]), token[1], int(token[2])
        if kind == "a":
            pass_on(k, i).wait_recv()

            @pl.when(passes(i))
            def _():
                pass_on(k, i).start()

            if full(i):
                send(k, i, *((1, 0) if k == 0 else (0, 1)))
                send(k, i, *((0, 1) if k == 0 else (1, 0)))
            else:
                send(k, i, *((0, 1) if k == 0 else (1, 0)))
            send(k, i, 0, 0, 1)
            return
        if kind == "x":
            extra_wait(k)
            send(EXTRA[k][0], i, *EXTRA[k][1:], 1)
            return
        first = (1, 0) if k == 0 else (0, 1)
        s, u = {"f": first, "g": first[::-1], "h": (1, 1)}[kind]
        gather_wait(k, i, s, u)
        if kind == "f":
            send(k, i, 1, 1)
        send(k, i, s, u, 1)

    atoms, rest = atoms_of(ORDER)
    wide = [atom for atom in atoms if atom["a"] == 0]
    tall = [atom for atom in atoms if atom["a"] == 1]

    def fb_at(index, group):
        return select(index, [layer[atom["i"]] * 2 + y_of(atom["s"]) for atom in group])

    def select(index, values):
        result = values[0]
        for k, value in enumerate(values[1:], 1):
            result = jnp.where(index >= k, value, result)
        return result

    return_fb = [fb_of(*item) for item in RETURN]

    def columns_of(fb):
        return pl.ds(pl.multiple_of(fb * width, width), width)

    def wide_copies(index, place):
        columns = columns_of(place)
        at = lax.rem(index, 2)
        return [
            pltpu.make_async_copy(ref.at[:, columns], wab.at[at, k], wasem.at[at, k])
            for k, ref in enumerate((wg_ref, wu_ref))
        ]

    def tall_copy(index, place):
        at = lax.rem(index, 2)
        return pltpu.make_async_copy(wd_ref.at[:, columns_of(place)], wb.at[at], wbsem.at[at])

    local = [
        pltpu.make_async_copy(x_ref, tok.at[0, fb_of(0, 0), e], lsem.at[0]),
        pltpu.make_async_copy(dy_ref, tok.at[1, fb_of(0, 0), e], lsem.at[1]),
    ]
    tables = [
        pltpu.make_async_copy(gain_hbm, gain_ref, lsem.at[3]),
        pltpu.make_async_copy(ids_hbm, ids_ref, lsem.at[4]),
        pltpu.make_async_copy(prob_hbm, prob_ref, lsem.at[5]),
    ]
    peers = [(e, lax.rem(z + d, T), y_of(s)) for d in range(T) for s in (0, 1) if d or s]
    sources = [fb_of(d, s) for d in range(T) for s in (0, 1) if d or s]
    others = [(lax.rem(e + k, 4), z, y) for k in (1, 2, 3)]
    barrier = pltpu.get_barrier_semaphore()
    for peer in peers + others:
        pl.semaphore_signal(barrier, inc=1, device_id=peer, device_id_type=MESH)
    for copy in tables + local:
        copy.start()
    pl.semaphore_wait(barrier, len(peers) + len(others))

    for a in (0, 1):
        for way in (0, 1):
            @pl.when(z < T - 1 if way else z > 0)
            def _():
                own_line(a, way).start()
    for item in ((0, 0, 1, 0), (1, 0, 0, 1), (0, 0, 0, 1), (1, 0, 1, 0), (0, 0, 0, 0, 1), (1, 0, 0, 0, 1)):
        send(*item)
    for copy in wide_copies(0, fb_at(0, wide)) + [tall_copy(0, fb_at(0, tall))]:
        copy.start()

    for copy in tables:
        copy.wait()
    number_of = lax.broadcasted_iota(jnp.int32, (8, tokens), 0)
    named_by = jnp.where(number_of < 4, number_of, number_of - 4)
    first = jnp.broadcast_to(ids_ref[0:1, :], (8, tokens)) == named_by
    second = jnp.broadcast_to(ids_ref[1:2, :], (8, tokens)) == named_by
    named = jnp.where(first, 1.0, 0.0) + jnp.where(second, 1.0, 0.0)
    later = (
        lax.broadcasted_iota(jnp.int32, (tokens, tokens), 0)
        < lax.broadcasted_iota(jnp.int32, (tokens, tokens), 1)
    )
    before = jnp.dot(
        named.astype(jnp.bfloat16), jnp.where(later, 1.0, 0.0).astype(jnp.bfloat16),
        preferred_element_type=jnp.float32,
    )
    weight = jnp.where(first, jnp.broadcast_to(prob_ref[0:1, :], (8, tokens)), 0.0) + jnp.where(
        second, jnp.broadcast_to(prob_ref[1:2, :], (8, tokens)), 0.0
    )
    own_meta[...] = jnp.where(number_of < 4, jnp.where(named > 0.0, before, -1.0), weight)
    metas[e] = own_meta[...]
    own_gain[...] = jnp.broadcast_to(gain_ref[...].astype(jnp.float32)[None, :], own_gain.shape)
    gains[fb_of(0, 0)] = own_gain[...]

    small = []
    for k, peer in enumerate(others):
        copy = remote(own_meta, metas.at[e], small_send.at[k], small_recv.at[k], peer)
        copy.start()
        there = metas.at[lax.rem(e + 3 - k, 4)]
        small.append((copy, remote(there, there, small_send.at[k], small_recv.at[k], peer)))
    for k, peer in enumerate(peers):
        n = 3 + k
        copy = remote(own_gain, gains.at[fb_of(0, 0)], small_send.at[n], small_recv.at[n], peer)
        copy.start()
        there = gains.at[sources[k]]
        small.append((copy, remote(there, there, small_send.at[n], small_recv.at[n], peer)))

    own_sq[...] = jnp.zeros_like(own_sq)
    ssq[...] = jnp.zeros_like(ssq)

    def clear(n, carry):
        for k in range(3):
            acc[k, n] = jnp.zeros(acc.shape[2:], jnp.float32)
        return carry

    lax.fori_loop(0, tiles, clear, 0)
    for copy, arrival in small[:3]:
        arrival.wait_recv()
    for b in range(4):
        slots = metas[b, pl.ds(e, 1), :]
        probs = metas[b, pl.ds(4 + e, 1), :]
        index = lax.broadcasted_iota(jnp.int32, (CAP, slots.shape[1]), 0).astype(jnp.float32)
        chosen = jnp.where(index == slots, 1.0, 0.0)
        sel[b] = chosen.astype(jnp.bfloat16)
        prob[pl.ds(b * CAP, CAP), :] = jnp.sum(chosen * probs, axis=1, keepdims=True)
    for copy, arrival in small[3:]:
        arrival.wait_recv()
    for copy in local:
        copy.wait()

    def accumulate(k, source, weights):
        for n in range(tiles):
            acc[k, n] += lax.dot_general(
                source[...], weights[n * TILE : (n + 1) * TILE, :], contract_width,
                preferred_element_type=jnp.float32,
            )

    def dispatch(index, low, high, run, used):
        if not any(k in used for k in range(low, high)):
            return
        if high - low == 1:
            run(low)
            return
        middle = (low + high) // 2
        for cond, first, last in ((index < middle, low, middle), (index >= middle, middle, high)):
            if any(k in used for k in range(first, last)):
                @pl.when(cond)
                def _():
                    dispatch(index, first, last, run, used)

    def gather_step(j, carry):
        def before_atom(k):
            for token in atoms[k]["ahead"]:
                event(token)
            for u in (0, 1):
                gather_wait(atoms[k]["a"], atoms[k]["i"], atoms[k]["s"], u, 1)

        def amid_atom(k):
            for token in atoms[k]["middle"]:
                event(token)

        dispatch(j, 0, len(atoms), before_atom, range(len(atoms)))

        kinds = [atom["a"] for atom in atoms]
        ranks = [sum(kinds[:k]) for k in range(len(atoms))]
        kind = pick(j, kinds)
        tall_rank = pick(j, ranks)
        wide_rank = j - tall_rank

        @pl.when(kind == 0)
        def _():
            following = jnp.where(
                wide_rank < BLOCKS - 1, fb_at(wide_rank + 1, wide), return_fb[0]
            )
            for copy in wide_copies(wide_rank + 1, following):
                copy.start()
            fb = fb_at(wide_rank, wide)
            gain_row = gains[fb, 0:1, :]
            mine = tok[0, fb, e].astype(jnp.float32)
            own_sq[...] += jnp.sum(mine * mine, axis=1, keepdims=True)
            for b in range(4):
                rows = pl.ds(b * CAP, CAP)
                picked = jnp.dot(sel[b], tok[0, fb, b], preferred_element_type=jnp.float32)
                ssq[rows, :] += jnp.sum(picked * picked, axis=1, keepdims=True)
                routed[0, rows, :] = (picked * gain_row).astype(jnp.bfloat16)
            for copy in wide_copies(wide_rank, fb):
                copy.wait()
            at = lax.rem(wide_rank, 2)
            accumulate(0, routed.at[0], wab.at[at, 0])
            dispatch(j, 0, len(atoms), amid_atom, [k for k, atom in enumerate(atoms) if atom["middle"]])
            accumulate(1, routed.at[0], wab.at[at, 1])

        @pl.when(kind == 1)
        def _():
            @pl.when(tall_rank < BLOCKS - 1)
            def _():
                tall_copy(tall_rank + 1, fb_at(tall_rank + 1, tall)).start()

            fb = fb_at(tall_rank, tall)
            for b in range(4):
                rows = pl.ds(b * CAP, CAP)
                picked = jnp.dot(sel[b], tok[1, fb, b], preferred_element_type=jnp.float32)
                routed[1, rows, :] = (picked * prob[rows, :]).astype(jnp.bfloat16)
            tall_copy(tall_rank, fb).wait()
            accumulate(2, routed.at[1], wb.at[lax.rem(tall_rank, 2)])

        return carry

    lax.fori_loop(0, len(atoms), gather_step, 0)
    for token in rest:
        event(token)
    reload = pltpu.make_async_copy(x_ref, own_x, lsem.at[2])
    reload.start()
    for item in sent:
        gather_copy(*item).wait_send()
    for a in (0, 1):
        for way in (0, 1):
            @pl.when(z < T - 1 if way else z > 0)
            def _():
                own_line(a, way).wait_send()
        for i in range(1, T):
            @pl.when(passes(i))
            def _():
                pass_on(a, i).wait_send()
    for k in range(len(EXTRA)):
        extra_copy(k).wait_send()
    for copy, arrival in small:
        copy.wait_send()

    inverse = lax.rsqrt(ssq[...] / D + epsilon)

    def activate(n, start):
        columns = pl.ds(pl.multiple_of(n * TILE, TILE), TILE)
        gate_sum, up_sum, act_grad = acc[0, n], acc[1, n], acc[2, n]
        gate_value = gate_sum * inverse
        up_value = up_sum * inverse
        sigmoid_gate = jax.nn.sigmoid(gate_value)
        gate_grad = (
            act_grad * up_value * sigmoid_gate * (1.0 + gate_value * (1.0 - sigmoid_gate))
        ).astype(jnp.bfloat16)
        up_grad = (act_grad * gate_value * sigmoid_gate).astype(jnp.bfloat16)
        hid[0, :, columns] = gate_grad
        hid[1, :, columns] = up_grad
        term = gate_grad.astype(jnp.float32) * gate_sum + up_grad.astype(jnp.float32) * up_sum
        acc[2, 0] = term if start else acc[2, 0] + term

    def activate_more(n, carry):
        activate(n, False)
        return carry

    activate(0, True)
    lax.fori_loop(1, tiles, activate_more, 0)

    def share_copies():
        return [
            remote(psend, precv.at[k], small_send.at[10 + k], small_recv.at[10 + k], peer)
            for k, peer in enumerate(peers)
        ]

    def total_copies():
        return [
            remote(ptotal, pothers.at[k], small_send.at[17 + k], small_recv.at[17 + k], peer)
            for k, peer in enumerate(others)
        ]

    def share_projection():
        pairs = jnp.sum(acc[2, 0], axis=1, keepdims=True)
        for b in range(4):
            of_block = sel[b].astype(jnp.float32) * pairs[b * CAP : (b + 1) * CAP]
            psend[b : b + 1, :] = jnp.sum(of_block, axis=0, keepdims=True)
        psend[4:8, :] = jnp.zeros((4, tokens), jnp.float32)
        for copy in share_copies():
            copy.start()

    def total_projection():
        for copy in share_copies():
            copy.wait_recv()
        row = psend[...]
        for k in range(len(peers)):
            row = row + precv[k]
        ptotal[...] = row
        for copy in total_copies():
            copy.start()

    def finish_projection():
        for copy in total_copies():
            copy.wait_recv()
        row = ptotal[pl.ds(e, 1), :]
        for k in range(len(others)):
            row = row + pothers[k, pl.ds(e, 1), :]
        projection = jnp.broadcast_to(row, (128, tokens)).T[:, 0:1]
        inverse = lax.rsqrt(own_sq[...] / D + epsilon)
        factor[...] = inverse * inverse * inverse * projection / D

    upper, lower = pl.ds(0, half), pl.ds(half, half)

    def core_copy(i, u):
        return remote(
            tok.at[0, i, lax.rem(core + 2 * u, 4)], crecv.at[i, u],
            rs_send.at[i, u], rs_recv.at[i, u], core_peer,
        )

    def across_copy(i, h):
        rows = lower if h else upper
        return remote(
            tok.at[1, i, 0, rows], xrecv.at[i, rows], rs_send.at[i, 2 + h], rs_recv.at[i, 2 + h], across_peer
        )

    def side_copy(i, u, h):
        d = RETURN[i][0]
        rows = lower if h else upper
        n = 4 + (u if h else 2)
        return remote(
            tok.at[1, i, 0 if u else 1, rows], yrecv.at[d, u, rows], rs_send.at[i, n], rs_recv.at[i, n], side_peer
        )

    def line_copy(i):
        d = RETURN[i][0]
        return remote(
            tok.at[1, i, 2], zrecv.at[d - 1], rs_send.at[i, 7], rs_recv.at[i, 7], (e, z_of(d), y)
        )

    def total(rows, *parts):
        value = parts[0][rows].astype(jnp.float32)
        for part in parts[1:]:
            value = value + part[rows].astype(jnp.float32)
        return value

    everything = pl.ds(0, tokens)

    def first_stage(i):
        core_copy(i, 1).wait_recv()
        far = (tok.at[0, i, across], crecv.at[i, 1])
        if RETURN[i][1]:
            tok[1, i, 0] = total(everything, *far).astype(jnp.bfloat16)
            across_copy(i, 0).start()
            side_copy(i, 1, 1).start()
            core_copy(i, 0).wait_recv()
            tok[1, i, 1, lower] = total(lower, tok.at[0, i, e], crecv.at[i, 0]).astype(jnp.bfloat16)
            side_copy(i, 0, 1).start()
        else:
            tok[1, i, 0, upper] = total(upper, *far).astype(jnp.bfloat16)
            across_copy(i, 0).start()

    def second_stage(i):
        d, s = RETURN[i]
        if s:
            across_copy(i, 0).wait_recv()
            tok[1, i, 1, upper] = total(
                upper, tok.at[0, i, e], crecv.at[i, 0], xrecv.at[i]
            ).astype(jnp.bfloat16)
            side_copy(i, 0, 0).start()
        else:
            side_copy(i - 1, 1, 1).wait_recv()
            tok[1, i, 0, lower] = total(
                lower, tok.at[0, i, across], crecv.at[i, 1], yrecv.at[d, 1]
            ).astype(jnp.bfloat16)
            across_copy(i, 1).start()

    def third_stage(i):
        d = RETURN[i][0]
        core_copy(i, 0).wait_recv()
        across_copy(i, 0).wait_recv()
        side_copy(i - 1, 0, 1).wait_recv()
        side_copy(i - 1, 0, 0).wait_recv()
        across_copy(i, 1).wait_recv()
        value = total(everything, tok.at[0, i, e], crecv.at[i, 0], xrecv.at[i], yrecv.at[d, 0])
        if d:
            tok[1, i, 2] = value.astype(jnp.bfloat16)
            line_copy(i).start()
        return value

    halves = width // TILE
    stages = {}
    for i, (d, s) in enumerate(RETURN):
        base = halves * (i + 1)
        plan = [(1, first_stage), (4, second_stage)] if s else [(1, first_stage), (2, second_stage), (5, third_stage)]
        for when, stage in plan:
            stages.setdefault(base + when, []).append((stage, i))

    def produce(h, carry):
        def run_stages(k):
            for stage, i in stages.get(k, []):
                stage(i)
            for when, step in ((2, share_projection), (8, total_projection), (14, finish_projection)):
                if k == when:
                    step()

        dispatch(h, 0, halves * BLOCKS, run_stages, [*stages, 2, 8, 14])

        i, n = h // halves, lax.rem(h, halves)

        @pl.when(jnp.logical_and(n == 0, i < BLOCKS - 1))
        def _():
            for copy in wide_copies(i + 1, select(i + 1, return_fb)):
                copy.start()

        @pl.when(n == 0)
        def _():
            for copy in wide_copies(i, select(i, return_fb)):
                copy.wait()

        at = lax.rem(i, 2)
        columns = pl.ds(pl.multiple_of(n * TILE, TILE), TILE)
        rounded = (
            jnp.dot(hid[0], wab[at, 0, :, columns], preferred_element_type=jnp.float32)
            + jnp.dot(hid[1], wab[at, 1, :, columns], preferred_element_type=jnp.float32)
        ).astype(jnp.bfloat16)
        for b in range(4):
            tok[0, i, b, :, columns] = lax.dot_general(
                sel[b], rounded[b * CAP : (b + 1) * CAP], contract_slots,
                preferred_element_type=jnp.float32,
            ).astype(jnp.bfloat16)

        @pl.when(n == halves - 1)
        def _():
            core_copy(i, 1).start()
            core_copy(i, 0).start()

        return carry

    lax.fori_loop(0, halves * BLOCKS, produce, 0)
    value = None
    for key in sorted(stages):
        if key >= halves * BLOCKS:
            for stage, i in stages[key]:
                value = stage(i)
    reload.wait()
    for i in range(BLOCKS):
        if RETURN[i][1] == 0 and RETURN[i][0]:
            line_copy(i).wait_recv()
            value = value + zrecv[RETURN[i][0] - 1].astype(jnp.float32)

    gain_row = gains[fb_of(0, 0), 0:1, :]
    stream = own_x[...].astype(jnp.float32)
    scaled = value * gain_row
    inverse = lax.rsqrt(own_sq[...] / D + epsilon)
    out_ref[...] = (inverse * scaled - stream * factor[...]).astype(out_ref.dtype)
    for copy in share_copies() + total_copies():
        copy.wait_send()
    for i, (d, s) in enumerate(RETURN):
        core_copy(i, 0).wait_send()
        core_copy(i, 1).wait_send()
        across_copy(i, 0).wait_send()
        if s:
            side_copy(i, 1, 1).wait_send()
            side_copy(i, 0, 1).wait_send()
            side_copy(i, 0, 0).wait_send()
        else:
            across_copy(i, 1).wait_send()
            if d:
                line_copy(i).wait_send()


def fused_shards(residual_stream, grad_output, norm_gain, expert_ids, gate_probs, w_gate, w_up, w_down):
    experts = lax.axis_size("expert")
    tokens, width = residual_stream.shape
    hidden = w_gate.shape[1]
    bf16, f32 = jnp.bfloat16, jnp.float32
    rows = experts * CAP
    vmem = pl.BlockSpec(memory_space=pltpu.VMEM)
    hbm = pl.BlockSpec(memory_space=pl.ANY)
    dma = pltpu.SemaphoreType.DMA
    unit = (tokens, width)
    smalls = 3 + 2 * (BLOCKS - 1) + 3
    return pl.pallas_call(
        fused_kernel,
        out_shape=jax.ShapeDtypeStruct(unit, bf16),
        in_specs=[hbm] * 8,
        out_specs=vmem,
        scratch_shapes=[
            pltpu.VMEM((2, BLOCKS, experts) + unit, bf16),
            pltpu.VMEM((3, hidden // TILE, rows, TILE), f32),
            pltpu.VMEM((2, 2, hidden, width), bf16),
            pltpu.VMEM((2, hidden, width), bf16),
            pltpu.VMEM((2, rows, hidden), bf16),
            pltpu.VMEM((2, rows, width), bf16),
            pltpu.VMEM((BLOCKS, 2) + unit, bf16),
            pltpu.VMEM((BLOCKS,) + unit, bf16),
            pltpu.VMEM((T, 2) + unit, bf16),
            pltpu.VMEM((T - 1,) + unit, bf16),
            pltpu.VMEM((BLOCKS, 8, width), f32),
            pltpu.VMEM((experts, 8, tokens), f32),
            pltpu.VMEM((experts, CAP, tokens), bf16),
            pltpu.VMEM((rows, 1), f32),
            pltpu.VMEM((rows, 1), f32),
            pltpu.VMEM((tokens, 1), f32),
            pltpu.VMEM((8, tokens), f32),
            pltpu.VMEM((BLOCKS - 1, 8, tokens), f32),
            pltpu.VMEM((8, tokens), f32),
            pltpu.VMEM((3, 8, tokens), f32),
            pltpu.VMEM((tokens, 1), f32),
            pltpu.VMEM(unit, bf16),
            pltpu.VMEM((8, width), f32),
            pltpu.VMEM((8, tokens), f32),
            pltpu.VMEM((width,), bf16),
            pltpu.VMEM((2, tokens), jnp.int32),
            pltpu.VMEM((2, tokens), f32),
            dma((16 * T,)),
            dma((16 * T,)),
            dma((2, T + 1)),
            dma((2, T)),
            dma((len(EXTRA),)),
            dma((len(EXTRA),)),
            dma((BLOCKS, 8)),
            dma((BLOCKS, 8)),
            dma((smalls,)),
            dma((smalls,)),
            dma((2, 2)),
            dma((2,)),
            dma((6,)),
        ],
        compiler_params=pltpu.CompilerParams(
            collective_id=0, has_side_effects=True, vmem_limit_bytes=66000000
        ),
        name="fused",
    )(
        residual_stream, grad_output, norm_gain, expert_ids.T, gate_probs.T,
        w_gate[0], w_up[0], w_down[0],
    )


def solution(mesh):
    placed = (
        P("expert", ("tensor", "kv")),
        P("expert", ("tensor", "kv")),
        P(("tensor", "kv")),
        P("expert", None),
        P("expert", None),
        P("expert", ("tensor", "kv"), None),
        P("expert", ("tensor", "kv"), None),
        P("expert", ("tensor", "kv"), None),
    )
    sizes = dict(mesh.shape)
    width = D // (sizes["tensor"] * sizes["kv"])
    body = fused_shards if sizes == {"expert": 4, "tensor": 4, "kv": 2} and width % 256 == 0 else shards
    return jax.shard_map(
        body, mesh=mesh, in_specs=placed, out_specs=P("expert", ("tensor", "kv")), check_vma=False
    )
```

```python
import functools

import jax
import jax.numpy as jnp
from jax import lax
from jax.experimental import pallas as pl
from jax.experimental.pallas import tpu as pltpu
from jax.sharding import PartitionSpec as P

D = 4096
CAP = 160


epsilon = 1e-05
contract_width = (((1,), (1,)), ((), ()))
contract_hidden = (((0,), (1,)), ((), ()))
contract_slots = (((0,), (0,)), ((), ()))


def slot_matrix(ids_block, experts):
    flattened = ids_block.reshape(-1)
    onehot = (flattened[:, None] == jnp.arange(experts, dtype=jnp.int32)[None, :]).astype(jnp.int32)
    before = jnp.cumsum(onehot, axis=0) - onehot
    position = jnp.sum(before * onehot, axis=1)
    slot_index = flattened * CAP + position
    table = jnp.arange(experts * CAP, dtype=jnp.int32)
    return (slot_index[None, :] == table[:, None]).astype(jnp.bfloat16)


def shards(residual_stream, grad_output, norm_gain, expert_ids, gate_probs, w_gate, w_up, w_down):
    experts = lax.axis_size("expert")
    local_width = residual_stream.shape[1]
    tokens_here = residual_stream.shape[0]
    stream = residual_stream.astype(jnp.float32)
    squares = lax.psum(jnp.sum(stream * stream, axis=1), ("tensor", "kv"))
    inverse_rms = lax.rsqrt(squares / D + epsilon)[:, None]
    gains = norm_gain.astype(jnp.float32)
    normed = (stream * inverse_rms * gains).astype(jnp.bfloat16)
    table = slot_matrix(expert_ids, experts)
    repeated_x = jnp.repeat(normed, 2, axis=0)
    scaled = (
        jnp.repeat(grad_output.astype(jnp.float32), 2, axis=0) * gate_probs.reshape(-1, 1)
    ).astype(jnp.bfloat16)
    routed_x = jnp.dot(table, repeated_x, preferred_element_type=jnp.float32).astype(jnp.bfloat16)
    routed_grad = jnp.dot(table, scaled, preferred_element_type=jnp.float32).astype(jnp.bfloat16)
    routed_x = routed_x.reshape(experts, CAP, local_width)
    routed_grad = routed_grad.reshape(experts, CAP, local_width)
    gate_weight, up_weight, down_weight = (w_gate[0], w_up[0], w_down[0])
    pieces_x = lax.all_to_all(routed_x, "expert", split_axis=0, concat_axis=0, tiled=True)
    pieces_dy = lax.all_to_all(routed_grad, "expert", split_axis=0, concat_axis=0, tiled=True)
    full_x = lax.all_gather(pieces_x, ("tensor", "kv"), axis=2, tiled=True)
    full_dy = lax.all_gather(pieces_dy, ("tensor", "kv"), axis=2, tiled=True)
    leading = full_x.shape[0]
    items = full_x.shape[1]
    matrix_x = full_x.reshape(leading * items, D)
    matrix_dy = full_dy.reshape(leading * items, D)
    gate_value = lax.dot_general(
        matrix_x, gate_weight, contract_width, preferred_element_type=jnp.float32
    )
    up_value = lax.dot_general(
        matrix_x, up_weight, contract_width, preferred_element_type=jnp.float32
    )
    act_grad = lax.dot_general(
        matrix_dy, down_weight, contract_width, preferred_element_type=jnp.float32
    )
    sigmoid_gate = jax.nn.sigmoid(gate_value)
    activated = gate_value * sigmoid_gate
    gate_grad = (
        act_grad * up_value * sigmoid_gate * (1.0 + gate_value * (1.0 - sigmoid_gate))
    ).astype(jnp.bfloat16)
    up_grad = (act_grad * activated).astype(jnp.bfloat16)
    total = lax.dot_general(
        gate_weight, gate_grad, contract_hidden, preferred_element_type=jnp.float32
    )
    summed = lax.psum_scatter(
        total
        + lax.dot_general(up_weight, up_grad, contract_hidden, preferred_element_type=jnp.float32),
        ("tensor", "kv"),
        scatter_dimension=0,
        tiled=True,
    )
    returned = summed.T.astype(jnp.bfloat16).reshape(leading, items, local_width)
    combined = lax.all_to_all(returned, "expert", split_axis=0, concat_axis=0, tiled=True)
    gathered = lax.dot_general(
        table,
        combined.reshape(experts * CAP, local_width),
        contract_slots,
        preferred_element_type=jnp.float32,
    )
    token_grad = gathered.reshape(tokens_here, 2, local_width).sum(axis=1)
    scaled_grad = token_grad * gains
    projection = lax.psum(jnp.sum(scaled_grad * stream, axis=1), ("tensor", "kv"))[:, None]
    result = inverse_rms * scaled_grad - stream * inverse_rms**3 * projection / D
    return result.astype(jnp.bfloat16)


MESH = pl.DeviceIdType.MESH
TILE = 256
T = 4
BLOCKS = 2 * T
ORDER = [
    "0f0", "1a0", "0f1", "2a0", "1a1", "0g0", "2a1", "C000", "0h0", "D00", "C100", "0g1", "0h1", "3a0", "C001",
    "D01", "1g0", "3a1", "2g0", "e2", "e0", "C010", "2f0", "2f1", "D10", "C020", "D20", "C120", "3g0", "1x2",
    "C101", "3f0", "e1", "1g1", "C030", "3f1", "1x0", "2g1", "D30", "C130", "e3", "2h0", "C110", "1x1", "C021",
    "2h1", "D21", "C011", "3h0", "D11", "C121", "3h1", "3g1", "1x3", "C031", "D31", "C111", "C131",
]

EXTRA = [(1, 0, 1), (0, 1, 0), (0, 1, 1), (1, 1, 1)]
RETURN = [(d, s) for d in (1, 2, 3, 0) for s in (1, 0)]


def atoms_of(order):
    atoms, ahead = [], []
    for token in order:
        if token[0] == "C":
            atoms.append(dict(a=int(token[1]), i=int(token[2]), s=int(token[3]), ahead=ahead, middle=[]))
            ahead = []
        elif token[0] == "D":
            atoms[-1]["middle"], ahead = ahead, []
        else:
            ahead.append(token)
    return atoms, ahead


def pick(index, values):
    result = jnp.int32(values[0])
    for k, value in enumerate(values[1:], 1):
        if value != values[k - 1]:
            result = jnp.where(index >= k, value, result)
    return result


def fused_kernel(
    x_ref, dy_ref, gain_hbm, ids_hbm, prob_hbm, wg_ref, wu_ref, wd_ref, out_hbm,
    tok, acc, wab, wb, hid, routed, crecv, xrecv, yrecv, zrecv, gains, metas, sel, prob,
    ssq, own_sq, own_inverse, psend, precv, ptotal, pothers, factor, own_x, own_gain, own_meta, gain_ref, ids_ref, prob_ref, out_ref,
    ag_send, ag_recv, line_send, line_recv, extra_send, extra_recv, rs_send, rs_recv,
    small_send, small_recv, wasem, wbsem, lsem,
):
    e = lax.axis_index("expert")
    z = lax.axis_index("tensor")
    y = lax.axis_index("kv")
    core = e + 1 - 2 * lax.rem(e, 2)
    across = lax.rem(e + 2, 4)
    partner = z + 1 - 2 * lax.rem(z, 2)
    tokens, width = out_ref.shape
    half = tokens // 2
    hidden = wg_ref.shape[0]
    tiles = hidden // TILE
    inputs = (x_ref, dy_ref)
    low = z < 2
    layer = [z, partner, jnp.where(low, 2, 1), jnp.where(low, 3, 0)]

    def z_of(d):
        return lax.rem(z + T - d, T)

    def y_of(s):
        return y if s == 0 else 1 - y

    def fb_of(d, s):
        return z_of(d) * 2 + y_of(s)

    def seen(i, s):
        return layer[i] * 2 + y_of(s)

    def b_of(u, c):
        base = core if c else e
        return lax.rem(base + 2 * u, 4)

    def remote(src, dst, send, recv, peer):
        return pltpu.make_async_remote_copy(
            src_ref=src, dst_ref=dst, send_sem=send, recv_sem=recv,
            device_id=peer, device_id_type=MESH,
        )

    def slot(a, i, s, u, c=0):
        return tok.at[a, seen(i, s), b_of(u, c)]

    def number(a, i, s, u, c):
        return (((a * T + i) * 2 + s) * 2 + u) * 2 + c

    across_peer, side_peer, core_peer = (across, z, y), (e, z, 1 - y), (core, z, y)

    def source(a, i, s, u):
        return inputs[a] if (i, s, u) == (0, 0, 0) else slot(a, i, s, u)

    def gather_copy(a, i, s, u, c=0):
        n = number(a, i, s, u, c)
        if c:
            src, there, peer = (s, u), slot(a, i, s, u), core_peer
        elif (u and not s) or (s and u and a == 0):
            src, peer = (s, 0), across_peer
            there = slot(a, i, s, 0)
        else:
            src, peer = (0, u), side_peer
            there = slot(a, i, 0, u)
        return remote(source(a, i, *src), there, ag_send.at[n], ag_recv.at[n], peer)

    def gather_wait(a, i, s, u, c=0):
        n = number(a, i, s, u, c)
        here = slot(a, i, s, u, c)
        remote(here, here, ag_send.at[n], ag_recv.at[n], core_peer).wait_recv()

    def extra_copy(k):
        a, s, u = EXTRA[k]
        here = slot(a, 0, s, u)
        return remote(here, here, extra_send.at[k], extra_recv.at[k], (e, partner, y))

    def extra_wait(k):
        a, s, u = EXTRA[k]
        here = slot(a, 1, s, u)
        remote(here, here, extra_send.at[k], extra_recv.at[k], (e, partner, y)).wait_recv()

    def own_line(a, way):
        return remote(
            inputs[a], tok.at[a, fb_of(0, 0), e], line_send.at[a, way], line_recv.at[a, z],
            (e, z + 2 * way - 1, y),
        )

    def pass_on(a, i):
        v = layer[i]
        here = slot(a, i, 0, 0)
        return remote(
            here, here, line_send.at[a, 1 + i], line_recv.at[a, v],
            (e, jnp.where(v < z, z + 1, z - 1), y),
        )

    def passes(i):
        return jnp.where(layer[i] < z, z < T - 1, z > 0)

    sent = []

    def send(*item):
        sent.append(item)
        gather_copy(*item).start()

    def full(i):
        return i != 1

    def event(token):
        if token[0] == "e":
            extra_copy(int(token[1])).start()
            return
        i, kind, k = int(token[0]), token[1], int(token[2])
        if kind == "a":
            pass_on(k, i).wait_recv()

            @pl.when(passes(i))
            def _():
                pass_on(k, i).start()

            if full(i):
                send(k, i, *((1, 0) if k == 0 else (0, 1)))
                send(k, i, *((0, 1) if k == 0 else (1, 0)))
            else:
                send(k, i, *((0, 1) if k == 0 else (1, 0)))
            send(k, i, 0, 0, 1)
            return
        if kind == "x":
            extra_wait(k)
            send(EXTRA[k][0], i, *EXTRA[k][1:], 1)
            return
        first = (1, 0) if k == 0 else (0, 1)
        s, u = {"f": first, "g": first[::-1], "h": (1, 1)}[kind]
        gather_wait(k, i, s, u)
        if kind == "f":
            send(k, i, 1, 1)
        send(k, i, s, u, 1)

    atoms, rest = atoms_of(ORDER)
    wide = [atom for atom in atoms if atom["a"] == 0]
    tall = [atom for atom in atoms if atom["a"] == 1]

    def fb_at(index, group):
        return select(index, [layer[atom["i"]] * 2 + y_of(atom["s"]) for atom in group])

    def select(index, values):
        result = values[0]
        for k, value in enumerate(values[1:], 1):
            result = jnp.where(index >= k, value, result)
        return result

    return_fb = [fb_of(*item) for item in RETURN]

    def columns_of(fb):
        return pl.ds(pl.multiple_of(fb * width, width), width)

    def wide_copies(index, place):
        columns = columns_of(place)
        at = lax.rem(index, 2)
        return [
            pltpu.make_async_copy(ref.at[:, columns], wab.at[at, k], wasem.at[at, k])
            for k, ref in enumerate((wg_ref, wu_ref))
        ]

    def tall_copy(index, place):
        at = lax.rem(index, 2)
        return pltpu.make_async_copy(wd_ref.at[:, columns_of(place)], wb.at[at], wbsem.at[at])

    local = [
        pltpu.make_async_copy(x_ref, tok.at[0, fb_of(0, 0), e], lsem.at[0]),
        pltpu.make_async_copy(dy_ref, tok.at[1, fb_of(0, 0), e], lsem.at[1]),
    ]
    tables = [
        pltpu.make_async_copy(gain_hbm, gain_ref, lsem.at[3]),
        pltpu.make_async_copy(ids_hbm, ids_ref, lsem.at[4]),
        pltpu.make_async_copy(prob_hbm, prob_ref, lsem.at[5]),
    ]
    peers = [(e, lax.rem(z + d, T), y_of(s)) for d in range(T) for s in (0, 1) if d or s]
    sources = [fb_of(d, s) for d in range(T) for s in (0, 1) if d or s]
    others = [(lax.rem(e + k, 4), z, y) for k in (1, 2, 3)]
    barrier = pltpu.get_barrier_semaphore()
    for peer in peers + others:
        pl.semaphore_signal(barrier, inc=1, device_id=peer, device_id_type=MESH)
    for copy in tables + local:
        copy.start()
    pl.semaphore_wait(barrier, len(peers) + len(others))

    for a in (0, 1):
        for way in (0, 1):
            @pl.when(z < T - 1 if way else z > 0)
            def _():
                own_line(a, way).start()
    for item in ((0, 0, 1, 0), (1, 0, 0, 1), (0, 0, 0, 1), (1, 0, 1, 0), (0, 0, 0, 0, 1), (1, 0, 0, 0, 1)):
        send(*item)
    for copy in wide_copies(0, fb_at(0, wide)) + [tall_copy(0, fb_at(0, tall))]:
        copy.start()

    for copy in tables:
        copy.wait()
    number_of = lax.broadcasted_iota(jnp.int32, (8, tokens), 0)
    named_by = jnp.where(number_of < 4, number_of, number_of - 4)
    first = jnp.broadcast_to(ids_ref[0:1, :], (8, tokens)) == named_by
    second = jnp.broadcast_to(ids_ref[1:2, :], (8, tokens)) == named_by
    named = jnp.where(first, 1.0, 0.0) + jnp.where(second, 1.0, 0.0)
    later = (
        lax.broadcasted_iota(jnp.int32, (tokens, tokens), 0)
        < lax.broadcasted_iota(jnp.int32, (tokens, tokens), 1)
    )
    before = jnp.dot(
        named.astype(jnp.bfloat16), jnp.where(later, 1.0, 0.0).astype(jnp.bfloat16),
        preferred_element_type=jnp.float32,
    )
    weight = jnp.where(first, jnp.broadcast_to(prob_ref[0:1, :], (8, tokens)), 0.0) + jnp.where(
        second, jnp.broadcast_to(prob_ref[1:2, :], (8, tokens)), 0.0
    )
    own_meta[...] = jnp.where(number_of < 4, jnp.where(named > 0.0, before, -1.0), weight)
    metas[e] = own_meta[...]
    own_gain[...] = jnp.broadcast_to(gain_ref[...].astype(jnp.float32)[None, :], own_gain.shape)
    gains[fb_of(0, 0)] = own_gain[...]

    small = []
    for k, peer in enumerate(others):
        copy = remote(own_meta, metas.at[e], small_send.at[k], small_recv.at[k], peer)
        copy.start()
        there = metas.at[lax.rem(e + 3 - k, 4)]
        small.append((copy, remote(there, there, small_send.at[k], small_recv.at[k], peer)))
    for k, peer in enumerate(peers):
        n = 3 + k
        copy = remote(own_gain, gains.at[fb_of(0, 0)], small_send.at[n], small_recv.at[n], peer)
        copy.start()
        there = gains.at[sources[k]]
        small.append((copy, remote(there, there, small_send.at[n], small_recv.at[n], peer)))

    own_sq[...] = jnp.zeros_like(own_sq)
    ssq[...] = jnp.zeros_like(ssq)

    def clear(n, carry):
        for k in range(3):
            acc[k, n] = jnp.zeros(acc.shape[2:], jnp.float32)
        return carry

    lax.fori_loop(0, tiles, clear, 0)
    for copy, arrival in small[:3]:
        arrival.wait_recv()
    for b in range(4):
        slots = metas[b, pl.ds(e, 1), :]
        probs = metas[b, pl.ds(4 + e, 1), :]
        index = lax.broadcasted_iota(jnp.int32, (CAP, slots.shape[1]), 0).astype(jnp.float32)
        chosen = jnp.where(index == slots, 1.0, 0.0)
        sel[b] = chosen.astype(jnp.bfloat16)
        prob[pl.ds(b * CAP, CAP), :] = jnp.sum(chosen * probs, axis=1, keepdims=True)
    for copy, arrival in small[3:]:
        arrival.wait_recv()
    for copy in local:
        copy.wait()

    def by_lane(value):
        square = value * value
        lanes = [square[:, k : k + 128] for k in range(0, width, 128)]
        return sum(lanes[1:], lanes[0])

    def accumulate(k, source, weights):
        for n in range(tiles):
            acc[k, n] += lax.dot_general(
                source[...], weights[n * TILE : (n + 1) * TILE, :], contract_width,
                preferred_element_type=jnp.float32,
            )

    def dispatch(index, low, high, run, used):
        if not any(k in used for k in range(low, high)):
            return
        if high - low == 1:
            run(low)
            return
        middle = (low + high) // 2
        for cond, first, last in ((index < middle, low, middle), (index >= middle, middle, high)):
            if any(k in used for k in range(first, last)):
                @pl.when(cond)
                def _():
                    dispatch(index, first, last, run, used)

    def gather_step(j, carry):
        def before_atom(k):
            for token in atoms[k]["ahead"]:
                event(token)
            for u in (0, 1):
                gather_wait(atoms[k]["a"], atoms[k]["i"], atoms[k]["s"], u, 1)

        def amid_atom(k):
            for token in atoms[k]["middle"]:
                event(token)

        dispatch(j, 0, len(atoms), before_atom, range(len(atoms)))

        kinds = [atom["a"] for atom in atoms]
        ranks = [sum(kinds[:k]) for k in range(len(atoms))]
        kind = pick(j, kinds)
        tall_rank = pick(j, ranks)
        wide_rank = j - tall_rank

        @pl.when(kind == 0)
        def _():
            following = jnp.where(
                wide_rank < BLOCKS - 1, fb_at(wide_rank + 1, wide), return_fb[0]
            )
            for copy in wide_copies(wide_rank + 1, following):
                copy.start()
            fb = fb_at(wide_rank, wide)
            gain_row = gains[fb, 0:1, :]
            mine = tok[0, fb, e].astype(jnp.float32)
            own_sq[...] += by_lane(mine)
            for b in range(4):
                rows = pl.ds(b * CAP, CAP)
                picked = jnp.dot(sel[b], tok[0, fb, b], preferred_element_type=jnp.float32)
                ssq[rows, :] += by_lane(picked)
                routed[0, rows, :] = (picked * gain_row).astype(jnp.bfloat16)
            for copy in wide_copies(wide_rank, fb):
                copy.wait()
            at = lax.rem(wide_rank, 2)
            accumulate(0, routed.at[0], wab.at[at, 0])
            dispatch(j, 0, len(atoms), amid_atom, [k for k, atom in enumerate(atoms) if atom["middle"]])
            accumulate(1, routed.at[0], wab.at[at, 1])

        @pl.when(kind == 1)
        def _():
            @pl.when(tall_rank < BLOCKS - 1)
            def _():
                tall_copy(tall_rank + 1, fb_at(tall_rank + 1, tall)).start()

            fb = fb_at(tall_rank, tall)
            for b in range(4):
                rows = pl.ds(b * CAP, CAP)
                picked = jnp.dot(sel[b], tok[1, fb, b], preferred_element_type=jnp.float32)
                routed[1, rows, :] = (picked * prob[rows, :]).astype(jnp.bfloat16)
            tall_copy(tall_rank, fb).wait()
            accumulate(2, routed.at[1], wb.at[lax.rem(tall_rank, 2)])

        return carry

    lax.fori_loop(0, len(atoms), gather_step, 0)
    for token in rest:
        event(token)
    reload = pltpu.make_async_copy(x_ref, own_x, lsem.at[2])
    reload.start()
    for item in sent:
        gather_copy(*item).wait_send()
    for a in (0, 1):
        for way in (0, 1):
            @pl.when(z < T - 1 if way else z > 0)
            def _():
                own_line(a, way).wait_send()
        for i in range(1, T):
            @pl.when(passes(i))
            def _():
                pass_on(a, i).wait_send()
    for k in range(len(EXTRA)):
        extra_copy(k).wait_send()
    for copy, arrival in small:
        copy.wait_send()

    inverse = lax.rsqrt(jnp.sum(ssq[...], axis=1, keepdims=True) / D + epsilon)

    def activate(n, start):
        columns = pl.ds(pl.multiple_of(n * TILE, TILE), TILE)
        gate_sum, up_sum, act_grad = acc[0, n], acc[1, n], acc[2, n]
        gate_value = gate_sum * inverse
        up_value = up_sum * inverse
        sigmoid_gate = jax.nn.sigmoid(gate_value)
        gate_grad = (
            act_grad * up_value * sigmoid_gate * (1.0 + gate_value * (1.0 - sigmoid_gate))
        ).astype(jnp.bfloat16)
        up_grad = (act_grad * gate_value * sigmoid_gate).astype(jnp.bfloat16)
        hid[0, :, columns] = gate_grad
        hid[1, :, columns] = up_grad
        term = gate_grad.astype(jnp.float32) * gate_sum + up_grad.astype(jnp.float32) * up_sum
        acc[2, 0] = term if start else acc[2, 0] + term

    def activate_more(n, carry):
        activate(n, False)
        return carry

    activate(0, True)
    lax.fori_loop(1, tiles, activate_more, 0)

    def share_copies():
        return [
            remote(psend, precv.at[k], small_send.at[10 + k], small_recv.at[10 + k], peer)
            for k, peer in enumerate(peers)
        ]

    def total_copies():
        return [
            remote(ptotal, pothers.at[k], small_send.at[17 + k], small_recv.at[17 + k], peer)
            for k, peer in enumerate(others)
        ]

    def share_projection():
        pairs = jnp.sum(acc[2, 0], axis=1, keepdims=True)
        for b in range(4):
            of_block = sel[b].astype(jnp.float32) * pairs[b * CAP : (b + 1) * CAP]
            psend[b : b + 1, :] = jnp.sum(of_block, axis=0, keepdims=True)
        psend[4:8, :] = jnp.zeros((4, tokens), jnp.float32)
        for copy in share_copies():
            copy.start()

    def total_projection():
        for copy in share_copies():
            copy.wait_recv()
        row = psend[...]
        for k in range(len(peers)):
            row = row + precv[k]
        ptotal[...] = row
        for copy in total_copies():
            copy.start()

    def finish_projection():
        for copy in total_copies():
            copy.wait_recv()
        row = ptotal[pl.ds(e, 1), :]
        for k in range(len(others)):
            row = row + pothers[k, pl.ds(e, 1), :]
        projection = jnp.broadcast_to(row, (128, tokens)).T[:, 0:1]
        inverse = lax.rsqrt(jnp.sum(own_sq[...], axis=1, keepdims=True) / D + epsilon)
        own_inverse[...] = inverse
        factor[...] = inverse * inverse * inverse * projection / D

    upper, lower, everything = pl.ds(0, half), pl.ds(half, half), pl.ds(0, tokens)
    halves = width // TILE

    def place(m):
        i, n = m // halves, m % halves
        return i, *RETURN[i], pl.ds(n * TILE, TILE)

    def core_copy(m, u):
        i, n = m // halves, m % halves
        columns = pl.ds(pl.multiple_of(n * TILE, TILE), TILE)
        return remote(
            tok.at[0, i, lax.rem(core + 2 * u, 4), :, columns], crecv.at[i, u, :, columns],
            rs_send.at[m, u], rs_recv.at[m, u], core_peer,
        )

    def across_copy(m, h):
        i, d, s, columns = place(m)
        rows = lower if h else upper
        return remote(
            tok.at[1, i, 0, rows, columns], xrecv.at[i, rows, columns],
            rs_send.at[m, 2 + h], rs_recv.at[m, 2 + h], across_peer,
        )

    def side_copy(m, u, h):
        i, d, s, columns = place(m)
        rows = lower if h else upper
        n = 4 + (u if h else 2)
        return remote(
            tok.at[1, i, 0 if u else 1, rows, columns], yrecv.at[d, u, rows, columns],
            rs_send.at[m, n], rs_recv.at[m, n], side_peer,
        )

    def line_copy(m):
        i, d, s, columns = place(m)
        return remote(
            tok.at[1, i, 2, :, columns], zrecv.at[d - 1, :, columns],
            rs_send.at[m, 7], rs_recv.at[m, 7], (e, z_of(d), y),
        )

    def total(rows, columns, *parts):
        value = parts[0][rows, columns].astype(jnp.float32)
        for part in parts[1:]:
            value = value + part[rows, columns].astype(jnp.float32)
        return value

    def first_stage(m):
        i, d, s, columns = place(m)
        core_copy(m, 1).wait_recv()
        far = (tok.at[0, i, across], crecv.at[i, 1])
        if s:
            tok[1, i, 0, :, columns] = total(everything, columns, *far).astype(jnp.bfloat16)
            across_copy(m, 0).start()
            side_copy(m, 1, 1).start()
            core_copy(m, 0).wait_recv()
            tok[1, i, 1, lower, columns] = total(
                lower, columns, tok.at[0, i, e], crecv.at[i, 0]
            ).astype(jnp.bfloat16)
            side_copy(m, 0, 1).start()
        else:
            tok[1, i, 0, upper, columns] = total(upper, columns, *far).astype(jnp.bfloat16)
            across_copy(m, 0).start()

    def second_stage(m):
        i, d, s, columns = place(m)
        if s:
            across_copy(m, 0).wait_recv()
            tok[1, i, 1, upper, columns] = total(
                upper, columns, tok.at[0, i, e], crecv.at[i, 0], xrecv.at[i]
            ).astype(jnp.bfloat16)
            side_copy(m, 0, 0).start()
        else:
            side_copy(m - halves, 1, 1).wait_recv()
            tok[1, i, 0, lower, columns] = total(
                lower, columns, tok.at[0, i, across], crecv.at[i, 1], yrecv.at[d, 1]
            ).astype(jnp.bfloat16)
            across_copy(m, 1).start()

    def third_stage(m):
        i, d, s, columns = place(m)
        core_copy(m, 0).wait_recv()
        across_copy(m, 0).wait_recv()
        side_copy(m - halves, 0, 1).wait_recv()
        side_copy(m - halves, 0, 0).wait_recv()
        across_copy(m, 1).wait_recv()
        value = total(everything, columns, tok.at[0, i, e], crecv.at[i, 0], xrecv.at[i], yrecv.at[d, 0])
        if d:
            tok[1, i, 2, :, columns] = value.astype(jnp.bfloat16)
            line_copy(m).start()
        else:
            acc[0, m % halves, everything, :] = value

    stages = {}
    for m in range(halves * BLOCKS):
        plan = [(1, first_stage), (4, second_stage)] if place(m)[2] else (
            [(1, first_stage), (2, second_stage), (5, third_stage)]
        )
        for when, stage in plan:
            stages.setdefault(m + 1 + when, []).append((stage, m))

    def produce(h, carry):
        def run_stages(k):
            for stage, i in stages.get(k, []):
                stage(i)
            for when, step in ((6, share_projection), (10, total_projection), (15, finish_projection)):
                if k == when:
                    step()

        dispatch(h, 0, halves * BLOCKS, run_stages, [*stages, 6, 10, 15])

        i, n = h // halves, lax.rem(h, halves)

        @pl.when(jnp.logical_and(n == 0, i < BLOCKS - 1))
        def _():
            for copy in wide_copies(i + 1, select(i + 1, return_fb)):
                copy.start()

        @pl.when(n == 0)
        def _():
            for copy in wide_copies(i, select(i, return_fb)):
                copy.wait()

        at = lax.rem(i, 2)
        columns = pl.ds(pl.multiple_of(n * TILE, TILE), TILE)
        rounded = (
            jnp.dot(hid[0], wab[at, 0, :, columns], preferred_element_type=jnp.float32)
            + jnp.dot(hid[1], wab[at, 1, :, columns], preferred_element_type=jnp.float32)
        ).astype(jnp.bfloat16)
        for b in range(4):
            tok[0, i, b, :, columns] = lax.dot_general(
                sel[b], rounded[b * CAP : (b + 1) * CAP], contract_slots,
                preferred_element_type=jnp.float32,
            ).astype(jnp.bfloat16)

        core_copy(h, 1).start()
        core_copy(h, 0).start()
        return carry

    lax.fori_loop(0, halves * BLOCKS, produce, 0)
    for key in sorted(stages):
        if key >= halves * BLOCKS:
            for stage, m in stages[key]:
                stage(m)
    reload.wait()
    for n in range(halves):
        columns = pl.ds(n * TILE, TILE)
        value = acc[0, n, everything, :]
        for i, (d, s) in enumerate(RETURN):
            if d and not s:
                line_copy(halves * i + n).wait_recv()
                value = value + zrecv[d - 1, :, columns].astype(jnp.float32)
        scaled = value * gains[fb_of(0, 0), 0:1, columns]
        stream = own_x[:, columns].astype(jnp.float32)
        out_ref[:, columns] = (own_inverse[...] * scaled - stream * factor[...]).astype(out_ref.dtype)
    written = pltpu.make_async_copy(out_ref, out_hbm, lsem.at[2])
    written.start()
    for copy in share_copies() + total_copies():
        copy.wait_send()
    for m in range(halves * BLOCKS):
        i, d, s, columns = place(m)
        core_copy(m, 0).wait_send()
        core_copy(m, 1).wait_send()
        across_copy(m, 0).wait_send()
        if s:
            side_copy(m, 1, 1).wait_send()
            side_copy(m, 0, 1).wait_send()
            side_copy(m, 0, 0).wait_send()
        else:
            across_copy(m, 1).wait_send()
            if d:
                line_copy(m).wait_send()
    written.wait()


def fused_shards(residual_stream, grad_output, norm_gain, expert_ids, gate_probs, w_gate, w_up, w_down):
    experts = lax.axis_size("expert")
    tokens, width = residual_stream.shape
    hidden = w_gate.shape[1]
    bf16, f32 = jnp.bfloat16, jnp.float32
    rows = experts * CAP
    hbm = pl.BlockSpec(memory_space=pl.ANY)
    dma = pltpu.SemaphoreType.DMA
    unit = (tokens, width)
    smalls = 3 + 2 * (BLOCKS - 1) + 3
    return pl.pallas_call(
        fused_kernel,
        out_shape=jax.ShapeDtypeStruct(unit, bf16),
        in_specs=[hbm] * 8,
        out_specs=hbm,
        scratch_shapes=[
            pltpu.VMEM((2, BLOCKS, experts) + unit, bf16),
            pltpu.VMEM((3, hidden // TILE, rows, TILE), f32),
            pltpu.VMEM((2, 2, hidden, width), bf16),
            pltpu.VMEM((2, hidden, width), bf16),
            pltpu.VMEM((2, rows, hidden), bf16),
            pltpu.VMEM((2, rows, width), bf16),
            pltpu.VMEM((BLOCKS, 2) + unit, bf16),
            pltpu.VMEM((BLOCKS,) + unit, bf16),
            pltpu.VMEM((T, 2) + unit, bf16),
            pltpu.VMEM((T - 1,) + unit, bf16),
            pltpu.VMEM((BLOCKS, 8, width), f32),
            pltpu.VMEM((experts, 8, tokens), f32),
            pltpu.VMEM((experts, CAP, tokens), bf16),
            pltpu.VMEM((rows, 1), f32),
            pltpu.VMEM((rows, 128), f32),
            pltpu.VMEM((tokens, 128), f32),
            pltpu.VMEM((tokens, 1), f32),
            pltpu.VMEM((8, tokens), f32),
            pltpu.VMEM((BLOCKS - 1, 8, tokens), f32),
            pltpu.VMEM((8, tokens), f32),
            pltpu.VMEM((3, 8, tokens), f32),
            pltpu.VMEM((tokens, 1), f32),
            pltpu.VMEM(unit, bf16),
            pltpu.VMEM((8, width), f32),
            pltpu.VMEM((8, tokens), f32),
            pltpu.VMEM((width,), bf16),
            pltpu.VMEM((2, tokens), jnp.int32),
            pltpu.VMEM((2, tokens), f32),
            pltpu.VMEM(unit, bf16),
            dma((16 * T,)),
            dma((16 * T,)),
            dma((2, T + 1)),
            dma((2, T)),
            dma((len(EXTRA),)),
            dma((len(EXTRA),)),
            dma((width // TILE * BLOCKS, 8)),
            dma((width // TILE * BLOCKS, 8)),
            dma((smalls,)),
            dma((smalls,)),
            dma((2, 2)),
            dma((2,)),
            dma((6,)),
        ],
        compiler_params=pltpu.CompilerParams(
            collective_id=0, has_side_effects=True, vmem_limit_bytes=66000000
        ),
        name="fused",
    )(
        residual_stream, grad_output, norm_gain, expert_ids.T, gate_probs.T,
        w_gate[0], w_up[0], w_down[0],
    )


def solution(mesh):
    placed = (
        P("expert", ("tensor", "kv")),
        P("expert", ("tensor", "kv")),
        P(("tensor", "kv")),
        P("expert", None),
        P("expert", None),
        P("expert", ("tensor", "kv"), None),
        P("expert", ("tensor", "kv"), None),
        P("expert", ("tensor", "kv"), None),
    )
    sizes = dict(mesh.shape)
    width = D // (sizes["tensor"] * sizes["kv"])
    body = fused_shards if sizes == {"expert": 4, "tensor": 4, "kv": 2} and width % 256 == 0 else shards
    return jax.shard_map(
        body, mesh=mesh, in_specs=placed, out_specs=P("expert", ("tensor", "kv")), check_vma=False
    )
```

```python
import functools

import jax
import jax.numpy as jnp
from jax import lax
from jax.experimental import pallas as pl
from jax.experimental.pallas import tpu as pltpu
from jax.sharding import PartitionSpec as P

D = 4096
CAP = 160


epsilon = 1e-05
contract_width = (((1,), (1,)), ((), ()))
contract_hidden = (((0,), (1,)), ((), ()))
contract_slots = (((0,), (0,)), ((), ()))


def slot_matrix(ids_block, experts):
    flattened = ids_block.reshape(-1)
    onehot = (flattened[:, None] == jnp.arange(experts, dtype=jnp.int32)[None, :]).astype(jnp.int32)
    before = jnp.cumsum(onehot, axis=0) - onehot
    position = jnp.sum(before * onehot, axis=1)
    slot_index = flattened * CAP + position
    table = jnp.arange(experts * CAP, dtype=jnp.int32)
    return (slot_index[None, :] == table[:, None]).astype(jnp.bfloat16)


def shards(residual_stream, grad_output, norm_gain, expert_ids, gate_probs, w_gate, w_up, w_down):
    experts = lax.axis_size("expert")
    local_width = residual_stream.shape[1]
    tokens_here = residual_stream.shape[0]
    stream = residual_stream.astype(jnp.float32)
    squares = lax.psum(jnp.sum(stream * stream, axis=1), ("tensor", "kv"))
    inverse_rms = lax.rsqrt(squares / D + epsilon)[:, None]
    gains = norm_gain.astype(jnp.float32)
    normed = (stream * inverse_rms * gains).astype(jnp.bfloat16)
    table = slot_matrix(expert_ids, experts)
    repeated_x = jnp.repeat(normed, 2, axis=0)
    scaled = (
        jnp.repeat(grad_output.astype(jnp.float32), 2, axis=0) * gate_probs.reshape(-1, 1)
    ).astype(jnp.bfloat16)
    routed_x = jnp.dot(table, repeated_x, preferred_element_type=jnp.float32).astype(jnp.bfloat16)
    routed_grad = jnp.dot(table, scaled, preferred_element_type=jnp.float32).astype(jnp.bfloat16)
    routed_x = routed_x.reshape(experts, CAP, local_width)
    routed_grad = routed_grad.reshape(experts, CAP, local_width)
    gate_weight, up_weight, down_weight = (w_gate[0], w_up[0], w_down[0])
    pieces_x = lax.all_to_all(routed_x, "expert", split_axis=0, concat_axis=0, tiled=True)
    pieces_dy = lax.all_to_all(routed_grad, "expert", split_axis=0, concat_axis=0, tiled=True)
    full_x = lax.all_gather(pieces_x, ("tensor", "kv"), axis=2, tiled=True)
    full_dy = lax.all_gather(pieces_dy, ("tensor", "kv"), axis=2, tiled=True)
    leading = full_x.shape[0]
    items = full_x.shape[1]
    matrix_x = full_x.reshape(leading * items, D)
    matrix_dy = full_dy.reshape(leading * items, D)
    gate_value = lax.dot_general(
        matrix_x, gate_weight, contract_width, preferred_element_type=jnp.float32
    )
    up_value = lax.dot_general(
        matrix_x, up_weight, contract_width, preferred_element_type=jnp.float32
    )
    act_grad = lax.dot_general(
        matrix_dy, down_weight, contract_width, preferred_element_type=jnp.float32
    )
    sigmoid_gate = jax.nn.sigmoid(gate_value)
    activated = gate_value * sigmoid_gate
    gate_grad = (
        act_grad * up_value * sigmoid_gate * (1.0 + gate_value * (1.0 - sigmoid_gate))
    ).astype(jnp.bfloat16)
    up_grad = (act_grad * activated).astype(jnp.bfloat16)
    total = lax.dot_general(
        gate_weight, gate_grad, contract_hidden, preferred_element_type=jnp.float32
    )
    summed = lax.psum_scatter(
        total
        + lax.dot_general(up_weight, up_grad, contract_hidden, preferred_element_type=jnp.float32),
        ("tensor", "kv"),
        scatter_dimension=0,
        tiled=True,
    )
    returned = summed.T.astype(jnp.bfloat16).reshape(leading, items, local_width)
    combined = lax.all_to_all(returned, "expert", split_axis=0, concat_axis=0, tiled=True)
    gathered = lax.dot_general(
        table,
        combined.reshape(experts * CAP, local_width),
        contract_slots,
        preferred_element_type=jnp.float32,
    )
    token_grad = gathered.reshape(tokens_here, 2, local_width).sum(axis=1)
    scaled_grad = token_grad * gains
    projection = lax.psum(jnp.sum(scaled_grad * stream, axis=1), ("tensor", "kv"))[:, None]
    result = inverse_rms * scaled_grad - stream * inverse_rms**3 * projection / D
    return result.astype(jnp.bfloat16)


MESH = pl.DeviceIdType.MESH
TILE = 256
T = 4
BLOCKS = 2 * T
ORDER = [
    "0f0", "1a0", "0f1", "2a0", "1a1", "0g0", "2a1", "C000", "0h0", "D00", "C100", "0g1", "0h1", "3a0", "C001",
    "D01", "1g0", "3a1", "2g0", "e2", "e0", "C010", "2f0", "2f1", "D10", "C020", "D20", "C120", "3g0", "1x2",
    "C101", "3f0", "e1", "1g1", "C030", "3f1", "1x0", "2g1", "D30", "C130", "e3", "2h0", "C110", "1x1", "C021",
    "2h1", "D21", "C011", "3h0", "D11", "C121", "3h1", "3g1", "1x3", "C031", "D31", "C111", "C131",
]

EXTRA = [(1, 0, 1), (0, 1, 0), (0, 1, 1), (1, 1, 1)]
RETURN = [(d, s) for d in (1, 2, 3, 0) for s in (1, 0)]


def atoms_of(order):
    atoms, ahead = [], []
    for token in order:
        if token[0] == "C":
            atoms.append(dict(a=int(token[1]), i=int(token[2]), s=int(token[3]), ahead=ahead, middle=[]))
            ahead = []
        elif token[0] == "D":
            atoms[-1]["middle"], ahead = ahead, []
        else:
            ahead.append(token)
    return atoms, ahead


def pick(index, values):
    result = jnp.int32(values[0])
    for k, value in enumerate(values[1:], 1):
        if value != values[k - 1]:
            result = jnp.where(index >= k, value, result)
    return result


def fused_kernel(
    x_ref, dy_ref, gain_hbm, ids_hbm, prob_hbm, wg_ref, wu_ref, wd_ref, out_hbm,
    tok, acc, wab, wb, hid, routed, crecv, xrecv, yrecv, zrecv, gains, metas, sel, prob,
    ssq, own_sq, own_inverse, psend, precv, ptotal, pothers, factor, own_x, own_gain, own_meta, gain_ref, ids_ref, prob_ref, out_ref,
    ag_send, ag_recv, line_send, line_recv, extra_send, extra_recv, rs_send, rs_recv,
    small_send, small_recv, wasem, wbsem, lsem,
):
    e = lax.axis_index("expert")
    z = lax.axis_index("tensor")
    y = lax.axis_index("kv")
    core = e + 1 - 2 * lax.rem(e, 2)
    across = lax.rem(e + 2, 4)
    partner = z + 1 - 2 * lax.rem(z, 2)
    tokens, width = out_ref.shape
    half = tokens // 2
    hidden = wg_ref.shape[0]
    tiles = hidden // TILE
    inputs = (x_ref, dy_ref)
    low = z < 2
    layer = [z, partner, jnp.where(low, 2, 1), jnp.where(low, 3, 0)]

    def z_of(d):
        return lax.rem(z + T - d, T)

    def y_of(s):
        return y if s == 0 else 1 - y

    def fb_of(d, s):
        return z_of(d) * 2 + y_of(s)

    def seen(i, s):
        return layer[i] * 2 + y_of(s)

    def b_of(u, c):
        base = core if c else e
        return lax.rem(base + 2 * u, 4)

    def remote(src, dst, send, recv, peer):
        return pltpu.make_async_remote_copy(
            src_ref=src, dst_ref=dst, send_sem=send, recv_sem=recv,
            device_id=peer, device_id_type=MESH,
        )

    def slot(a, i, s, u, c=0):
        return tok.at[a, seen(i, s), b_of(u, c)]

    def number(a, i, s, u, c):
        return (((a * T + i) * 2 + s) * 2 + u) * 2 + c

    across_peer, side_peer, core_peer = (across, z, y), (e, z, 1 - y), (core, z, y)

    def source(a, i, s, u):
        return inputs[a] if (i, s, u) == (0, 0, 0) else slot(a, i, s, u)

    def gather_copy(a, i, s, u, c=0):
        n = number(a, i, s, u, c)
        if c:
            src, there, peer = (s, u), slot(a, i, s, u), core_peer
        elif (u and not s) or (s and u and a == 0):
            src, peer = (s, 0), across_peer
            there = slot(a, i, s, 0)
        else:
            src, peer = (0, u), side_peer
            there = slot(a, i, 0, u)
        return remote(source(a, i, *src), there, ag_send.at[n], ag_recv.at[n], peer)

    def gather_wait(a, i, s, u, c=0):
        n = number(a, i, s, u, c)
        here = slot(a, i, s, u, c)
        remote(here, here, ag_send.at[n], ag_recv.at[n], core_peer).wait_recv()

    def extra_copy(k):
        a, s, u = EXTRA[k]
        here = slot(a, 0, s, u)
        return remote(here, here, extra_send.at[k], extra_recv.at[k], (e, partner, y))

    def extra_wait(k):
        a, s, u = EXTRA[k]
        here = slot(a, 1, s, u)
        remote(here, here, extra_send.at[k], extra_recv.at[k], (e, partner, y)).wait_recv()

    def own_line(a, way):
        return remote(
            inputs[a], tok.at[a, fb_of(0, 0), e], line_send.at[a, way], line_recv.at[a, z],
            (e, z + 2 * way - 1, y),
        )

    def pass_on(a, i):
        v = layer[i]
        here = slot(a, i, 0, 0)
        return remote(
            here, here, line_send.at[a, 1 + i], line_recv.at[a, v],
            (e, jnp.where(v < z, z + 1, z - 1), y),
        )

    def passes(i):
        return jnp.where(layer[i] < z, z < T - 1, z > 0)

    sent = []

    def send(*item):
        sent.append(item)
        gather_copy(*item).start()

    def full(i):
        return i != 1

    def event(token):
        if token[0] == "e":
            extra_copy(int(token[1])).start()
            return
        i, kind, k = int(token[0]), token[1], int(token[2])
        if kind == "a":
            pass_on(k, i).wait_recv()

            @pl.when(passes(i))
            def _():
                pass_on(k, i).start()

            if full(i):
                send(k, i, *((1, 0) if k == 0 else (0, 1)))
                send(k, i, *((0, 1) if k == 0 else (1, 0)))
            else:
                send(k, i, *((0, 1) if k == 0 else (1, 0)))
            send(k, i, 0, 0, 1)
            return
        if kind == "x":
            extra_wait(k)
            send(EXTRA[k][0], i, *EXTRA[k][1:], 1)
            return
        first = (1, 0) if k == 0 else (0, 1)
        s, u = {"f": first, "g": first[::-1], "h": (1, 1)}[kind]
        gather_wait(k, i, s, u)
        if kind == "f":
            send(k, i, 1, 1)
        send(k, i, s, u, 1)

    atoms, rest = atoms_of(ORDER)
    wide = [atom for atom in atoms if atom["a"] == 0]
    tall = [atom for atom in atoms if atom["a"] == 1]

    def fb_at(index, group):
        return select(index, [layer[atom["i"]] * 2 + y_of(atom["s"]) for atom in group])

    def select(index, values):
        result = values[0]
        for k, value in enumerate(values[1:], 1):
            result = jnp.where(index >= k, value, result)
        return result

    return_fb = [fb_of(*item) for item in RETURN]

    def columns_of(fb):
        return pl.ds(pl.multiple_of(fb * width, width), width)

    def wide_copies(index, place):
        columns = columns_of(place)
        at = lax.rem(index, 2)
        return [
            pltpu.make_async_copy(ref.at[:, columns], wab.at[at, k], wasem.at[at, k])
            for k, ref in enumerate((wg_ref, wu_ref))
        ]

    def tall_copy(index, place):
        at = lax.rem(index, 2)
        return pltpu.make_async_copy(wd_ref.at[:, columns_of(place)], wb.at[at], wbsem.at[at])

    local = [
        pltpu.make_async_copy(x_ref, tok.at[0, fb_of(0, 0), e], lsem.at[0]),
        pltpu.make_async_copy(dy_ref, tok.at[1, fb_of(0, 0), e], lsem.at[1]),
    ]
    tables = [
        pltpu.make_async_copy(gain_hbm, gain_ref, lsem.at[3]),
        pltpu.make_async_copy(ids_hbm, ids_ref, lsem.at[4]),
        pltpu.make_async_copy(prob_hbm, prob_ref, lsem.at[5]),
    ]
    peers = [(e, lax.rem(z + d, T), y_of(s)) for d in range(T) for s in (0, 1) if d or s]
    sources = [fb_of(d, s) for d in range(T) for s in (0, 1) if d or s]
    others = [(lax.rem(e + k, 4), z, y) for k in (1, 2, 3)]
    barrier = pltpu.get_barrier_semaphore()
    for peer in peers + others:
        pl.semaphore_signal(barrier, inc=1, device_id=peer, device_id_type=MESH)
    for copy in tables + local:
        copy.start()
    pl.semaphore_wait(barrier, len(peers) + len(others))

    for a in (0, 1):
        for way in (0, 1):
            @pl.when(z < T - 1 if way else z > 0)
            def _():
                own_line(a, way).start()
    for item in ((0, 0, 1, 0), (1, 0, 0, 1), (0, 0, 0, 1), (1, 0, 1, 0), (0, 0, 0, 0, 1), (1, 0, 0, 0, 1)):
        send(*item)
    for copy in wide_copies(0, fb_at(0, wide)) + [tall_copy(0, fb_at(0, tall))]:
        copy.start()

    for copy in tables:
        copy.wait()
    number_of = lax.broadcasted_iota(jnp.int32, (8, tokens), 0)
    named_by = jnp.where(number_of < 4, number_of, number_of - 4)
    first = jnp.broadcast_to(ids_ref[0:1, :], (8, tokens)) == named_by
    second = jnp.broadcast_to(ids_ref[1:2, :], (8, tokens)) == named_by
    named = jnp.where(first, 1.0, 0.0) + jnp.where(second, 1.0, 0.0)
    later = (
        lax.broadcasted_iota(jnp.int32, (tokens, tokens), 0)
        < lax.broadcasted_iota(jnp.int32, (tokens, tokens), 1)
    )
    before = jnp.dot(
        named.astype(jnp.bfloat16), jnp.where(later, 1.0, 0.0).astype(jnp.bfloat16),
        preferred_element_type=jnp.float32,
    )
    weight = jnp.where(first, jnp.broadcast_to(prob_ref[0:1, :], (8, tokens)), 0.0) + jnp.where(
        second, jnp.broadcast_to(prob_ref[1:2, :], (8, tokens)), 0.0
    )
    own_meta[...] = jnp.where(number_of < 4, jnp.where(named > 0.0, before, -1.0), weight)
    metas[e] = own_meta[...]
    own_gain[...] = jnp.broadcast_to(gain_ref[...].astype(jnp.float32)[None, :], own_gain.shape)
    gains[fb_of(0, 0)] = own_gain[...]

    small = []
    for k, peer in enumerate(others):
        copy = remote(own_meta, metas.at[e], small_send.at[k], small_recv.at[k], peer)
        copy.start()
        there = metas.at[lax.rem(e + 3 - k, 4)]
        small.append((copy, remote(there, there, small_send.at[k], small_recv.at[k], peer)))
    for k, peer in enumerate(peers):
        n = 3 + k
        copy = remote(own_gain, gains.at[fb_of(0, 0)], small_send.at[n], small_recv.at[n], peer)
        copy.start()
        there = gains.at[sources[k]]
        small.append((copy, remote(there, there, small_send.at[n], small_recv.at[n], peer)))

    own_sq[...] = jnp.zeros_like(own_sq)
    ssq[...] = jnp.zeros_like(ssq)

    def clear(n, carry):
        for k in range(3):
            acc[k, n] = jnp.zeros(acc.shape[2:], jnp.float32)
        return carry

    lax.fori_loop(0, tiles, clear, 0)
    for copy, arrival in small[:3]:
        arrival.wait_recv()
    for b in range(4):
        slots = metas[b, pl.ds(e, 1), :]
        probs = metas[b, pl.ds(4 + e, 1), :]
        index = lax.broadcasted_iota(jnp.int32, (CAP, slots.shape[1]), 0).astype(jnp.float32)
        chosen = jnp.where(index == slots, 1.0, 0.0)
        sel[b] = chosen.astype(jnp.bfloat16)
        prob[pl.ds(b * CAP, CAP), :] = jnp.sum(chosen * probs, axis=1, keepdims=True)
    for copy, arrival in small[3:]:
        arrival.wait_recv()
    for copy in local:
        copy.wait()

    def by_lane(value):
        square = value * value
        lanes = [square[:, k : k + 128] for k in range(0, width, 128)]
        return sum(lanes[1:], lanes[0])

    def accumulate(k, source, weights):
        for n in range(tiles):
            acc[k, n] += lax.dot_general(
                source[...], weights[n * TILE : (n + 1) * TILE, :], contract_width,
                preferred_element_type=jnp.float32,
            )

    def dispatch(index, low, high, run, used):
        if not any(k in used for k in range(low, high)):
            return
        if high - low == 1:
            run(low)
            return
        middle = (low + high) // 2
        for cond, first, last in ((index < middle, low, middle), (index >= middle, middle, high)):
            if any(k in used for k in range(first, last)):
                @pl.when(cond)
                def _():
                    dispatch(index, first, last, run, used)

    def gather_step(j, carry):
        def before_atom(k):
            for token in atoms[k]["ahead"]:
                event(token)
            for u in (0, 1):
                gather_wait(atoms[k]["a"], atoms[k]["i"], atoms[k]["s"], u, 1)

        def amid_atom(k):
            for token in atoms[k]["middle"]:
                event(token)

        dispatch(j, 0, len(atoms), before_atom, range(len(atoms)))

        kinds = [atom["a"] for atom in atoms]
        ranks = [sum(kinds[:k]) for k in range(len(atoms))]
        kind = pick(j, kinds)
        tall_rank = pick(j, ranks)
        wide_rank = j - tall_rank

        @pl.when(kind == 0)
        def _():
            following = jnp.where(
                wide_rank < BLOCKS - 1, fb_at(wide_rank + 1, wide), return_fb[0]
            )
            for copy in wide_copies(wide_rank + 1, following):
                copy.start()
            fb = fb_at(wide_rank, wide)
            gain_row = gains[fb, 0:1, :]
            mine = tok[0, fb, e].astype(jnp.float32)
            own_sq[...] += by_lane(mine)
            for b in range(4):
                rows = pl.ds(b * CAP, CAP)
                picked = jnp.dot(sel[b], tok[0, fb, b], preferred_element_type=jnp.float32)
                ssq[rows, :] += by_lane(picked)
                routed[0, rows, :] = (picked * gain_row).astype(jnp.bfloat16)
            for copy in wide_copies(wide_rank, fb):
                copy.wait()
            at = lax.rem(wide_rank, 2)
            accumulate(0, routed.at[0], wab.at[at, 0])
            dispatch(j, 0, len(atoms), amid_atom, [k for k, atom in enumerate(atoms) if atom["middle"]])
            accumulate(1, routed.at[0], wab.at[at, 1])

        @pl.when(kind == 1)
        def _():
            @pl.when(tall_rank < BLOCKS - 1)
            def _():
                tall_copy(tall_rank + 1, fb_at(tall_rank + 1, tall)).start()

            fb = fb_at(tall_rank, tall)
            for b in range(4):
                rows = pl.ds(b * CAP, CAP)
                picked = jnp.dot(sel[b], tok[1, fb, b], preferred_element_type=jnp.float32)
                routed[1, rows, :] = (picked * prob[rows, :]).astype(jnp.bfloat16)
            tall_copy(tall_rank, fb).wait()
            accumulate(2, routed.at[1], wb.at[lax.rem(tall_rank, 2)])

        return carry

    lax.fori_loop(0, len(atoms), gather_step, 0)
    for token in rest:
        event(token)
    reload = pltpu.make_async_copy(x_ref, own_x, lsem.at[2])
    reload.start()
    for item in sent:
        gather_copy(*item).wait_send()
    for a in (0, 1):
        for way in (0, 1):
            @pl.when(z < T - 1 if way else z > 0)
            def _():
                own_line(a, way).wait_send()
        for i in range(1, T):
            @pl.when(passes(i))
            def _():
                pass_on(a, i).wait_send()
    for k in range(len(EXTRA)):
        extra_copy(k).wait_send()
    for copy, arrival in small:
        copy.wait_send()

    inverse = lax.rsqrt(jnp.sum(ssq[...], axis=1, keepdims=True) / D + epsilon)

    def activate(n, start):
        columns = pl.ds(pl.multiple_of(n * TILE, TILE), TILE)
        gate_sum, up_sum, act_grad = acc[0, n], acc[1, n], acc[2, n]
        gate_value = gate_sum * inverse
        up_value = up_sum * inverse
        sigmoid_gate = jax.nn.sigmoid(gate_value)
        gate_grad = (
            act_grad * up_value * sigmoid_gate * (1.0 + gate_value * (1.0 - sigmoid_gate))
        ).astype(jnp.bfloat16)
        up_grad = (act_grad * gate_value * sigmoid_gate).astype(jnp.bfloat16)
        hid[0, :, columns] = gate_grad
        hid[1, :, columns] = up_grad
        term = gate_grad.astype(jnp.float32) * gate_sum + up_grad.astype(jnp.float32) * up_sum
        acc[2, 0] = term if start else acc[2, 0] + term

    def activate_more(n, carry):
        activate(n, False)
        return carry

    activate(0, True)
    lax.fori_loop(1, tiles, activate_more, 0)

    def share_copies():
        return [
            remote(psend, precv.at[k], small_send.at[10 + k], small_recv.at[10 + k], peer)
            for k, peer in enumerate(peers)
        ]

    def total_copies():
        return [
            remote(ptotal, pothers.at[k], small_send.at[17 + k], small_recv.at[17 + k], peer)
            for k, peer in enumerate(others)
        ]

    def share_projection():
        pairs = jnp.sum(acc[2, 0], axis=1, keepdims=True)
        for b in range(4):
            of_block = sel[b].astype(jnp.float32) * pairs[b * CAP : (b + 1) * CAP]
            psend[b : b + 1, :] = jnp.sum(of_block, axis=0, keepdims=True)
        psend[4:8, :] = jnp.zeros((4, tokens), jnp.float32)
        for copy in share_copies():
            copy.start()

    def total_projection():
        for copy in share_copies():
            copy.wait_recv()
        row = psend[...]
        for k in range(len(peers)):
            row = row + precv[k]
        ptotal[...] = row
        for copy in total_copies():
            copy.start()

    def finish_projection():
        for copy in total_copies():
            copy.wait_recv()
        row = ptotal[pl.ds(e, 1), :]
        for k in range(len(others)):
            row = row + pothers[k, pl.ds(e, 1), :]
        projection = jnp.broadcast_to(row, (128, tokens)).T[:, 0:1]
        inverse = lax.rsqrt(jnp.sum(own_sq[...], axis=1, keepdims=True) / D + epsilon)
        own_inverse[...] = inverse
        factor[...] = inverse * inverse * inverse * projection / D

    upper, lower, everything = pl.ds(0, half), pl.ds(half, half), pl.ds(0, tokens)
    halves = width // TILE

    def place(m):
        i, n = m // halves, m % halves
        return i, *RETURN[i], pl.ds(n * TILE, TILE)

    def core_copy(m, u):
        i, n = m // halves, m % halves
        columns = pl.ds(pl.multiple_of(n * TILE, TILE), TILE)
        return remote(
            tok.at[0, i, lax.rem(core + 2 * u, 4), :, columns], crecv.at[i, u, :, columns],
            rs_send.at[m, u], rs_recv.at[m, u], core_peer,
        )

    def across_copy(m, h):
        i, d, s, columns = place(m)
        rows = lower if h else upper
        return remote(
            tok.at[1, i, 0, rows, columns], xrecv.at[i, rows, columns],
            rs_send.at[m, 2 + h], rs_recv.at[m, 2 + h], across_peer,
        )

    def side_copy(m, u, h):
        i, d, s, columns = place(m)
        rows = lower if h else upper
        n = 4 + (u if h else 2)
        return remote(
            tok.at[1, i, 0 if u else 1, rows, columns], yrecv.at[d, u, rows, columns],
            rs_send.at[m, n], rs_recv.at[m, n], side_peer,
        )

    def line_copy(m):
        i, d, s, columns = place(m)
        return remote(
            tok.at[1, i, 2, :, columns], zrecv.at[d - 1, :, columns],
            rs_send.at[m, 7], rs_recv.at[m, 7], (e, z_of(d), y),
        )

    def total(rows, columns, *parts):
        value = parts[0][rows, columns].astype(jnp.float32)
        for part in parts[1:]:
            value = value + part[rows, columns].astype(jnp.float32)
        return value

    def first_stage(m):
        i, d, s, columns = place(m)
        core_copy(m, 1).wait_recv()
        far = (tok.at[0, i, across], crecv.at[i, 1])
        if s:
            tok[1, i, 0, :, columns] = total(everything, columns, *far).astype(jnp.bfloat16)
            across_copy(m, 0).start()
            side_copy(m, 1, 1).start()
            core_copy(m, 0).wait_recv()
            tok[1, i, 1, lower, columns] = total(
                lower, columns, tok.at[0, i, e], crecv.at[i, 0]
            ).astype(jnp.bfloat16)
            side_copy(m, 0, 1).start()
        else:
            tok[1, i, 0, upper, columns] = total(upper, columns, *far).astype(jnp.bfloat16)
            across_copy(m, 0).start()

    def second_stage(m):
        i, d, s, columns = place(m)
        if s:
            across_copy(m, 0).wait_recv()
            tok[1, i, 1, upper, columns] = total(
                upper, columns, tok.at[0, i, e], crecv.at[i, 0], xrecv.at[i]
            ).astype(jnp.bfloat16)
            side_copy(m, 0, 0).start()
        else:
            side_copy(m - halves, 1, 1).wait_recv()
            tok[1, i, 0, lower, columns] = total(
                lower, columns, tok.at[0, i, across], crecv.at[i, 1], yrecv.at[d, 1]
            ).astype(jnp.bfloat16)
            across_copy(m, 1).start()

    def third_stage(m):
        i, d, s, columns = place(m)
        core_copy(m, 0).wait_recv()
        across_copy(m, 0).wait_recv()
        side_copy(m - halves, 0, 1).wait_recv()
        side_copy(m - halves, 0, 0).wait_recv()
        across_copy(m, 1).wait_recv()
        value = total(everything, columns, tok.at[0, i, e], crecv.at[i, 0], xrecv.at[i], yrecv.at[d, 0])
        if d:
            tok[1, i, 2, :, columns] = value.astype(jnp.bfloat16)
            line_copy(m).start()
        else:
            acc[0, m % halves, everything, :] = value

    stages = {}
    for m in range(halves * BLOCKS):
        plan = [(1, first_stage), (4, second_stage)] if place(m)[2] else (
            [(1, first_stage), (2, second_stage), (5, third_stage)]
        )
        for when, stage in plan:
            stages.setdefault(m + 1 + when, []).append((stage, m))

    projection_steps = {2: share_projection, 9: total_projection, 15: finish_projection}

    def run_stages(k):
        for stage, m in stages.get(k, []):
            stage(m)
        if k in projection_steps:
            projection_steps[k]()

    def produce(h, carry):

        dispatch(h, 0, halves * BLOCKS, run_stages, [*stages, *projection_steps])

        i, n = h // halves, lax.rem(h, halves)

        @pl.when(jnp.logical_and(n == 0, i < BLOCKS - 1))
        def _():
            for copy in wide_copies(i + 1, select(i + 1, return_fb)):
                copy.start()

        @pl.when(n == 0)
        def _():
            for copy in wide_copies(i, select(i, return_fb)):
                copy.wait()

        at = lax.rem(i, 2)
        columns = pl.ds(pl.multiple_of(n * TILE, TILE), TILE)
        rounded = (
            jnp.dot(hid[0], wab[at, 0, :, columns], preferred_element_type=jnp.float32)
            + jnp.dot(hid[1], wab[at, 1, :, columns], preferred_element_type=jnp.float32)
        ).astype(jnp.bfloat16)
        for b in range(4):
            tok[0, i, b, :, columns] = lax.dot_general(
                sel[b], rounded[b * CAP : (b + 1) * CAP], contract_slots,
                preferred_element_type=jnp.float32,
            ).astype(jnp.bfloat16)

        core_copy(h, 1).start()
        core_copy(h, 0).start()
        return carry

    lax.fori_loop(0, halves * BLOCKS, produce, 0)
    for key in sorted({*stages, *projection_steps}):
        if key >= halves * BLOCKS:
            run_stages(key)
    reload.wait()
    for n in range(halves):
        columns = pl.ds(n * TILE, TILE)
        value = acc[0, n, everything, :]
        for i, (d, s) in enumerate(RETURN):
            if d and not s:
                line_copy(halves * i + n).wait_recv()
                value = value + zrecv[d - 1, :, columns].astype(jnp.float32)
        scaled = value * gains[fb_of(0, 0), 0:1, columns]
        stream = own_x[:, columns].astype(jnp.float32)
        out_ref[:, columns] = (own_inverse[...] * scaled - stream * factor[...]).astype(out_ref.dtype)
    written = pltpu.make_async_copy(out_ref, out_hbm, lsem.at[2])
    written.start()
    for copy in share_copies() + total_copies():
        copy.wait_send()
    for m in range(halves * BLOCKS):
        i, d, s, columns = place(m)
        core_copy(m, 0).wait_send()
        core_copy(m, 1).wait_send()
        across_copy(m, 0).wait_send()
        if s:
            side_copy(m, 1, 1).wait_send()
            side_copy(m, 0, 1).wait_send()
            side_copy(m, 0, 0).wait_send()
        else:
            across_copy(m, 1).wait_send()
            if d:
                line_copy(m).wait_send()
    written.wait()


def fused_shards(residual_stream, grad_output, norm_gain, expert_ids, gate_probs, w_gate, w_up, w_down):
    experts = lax.axis_size("expert")
    tokens, width = residual_stream.shape
    hidden = w_gate.shape[1]
    bf16, f32 = jnp.bfloat16, jnp.float32
    rows = experts * CAP
    hbm = pl.BlockSpec(memory_space=pl.ANY)
    dma = pltpu.SemaphoreType.DMA
    unit = (tokens, width)
    smalls = 3 + 2 * (BLOCKS - 1) + 3
    return pl.pallas_call(
        fused_kernel,
        out_shape=jax.ShapeDtypeStruct(unit, bf16),
        in_specs=[hbm] * 8,
        out_specs=hbm,
        scratch_shapes=[
            pltpu.VMEM((2, BLOCKS, experts) + unit, bf16),
            pltpu.VMEM((3, hidden // TILE, rows, TILE), f32),
            pltpu.VMEM((2, 2, hidden, width), bf16),
            pltpu.VMEM((2, hidden, width), bf16),
            pltpu.VMEM((2, rows, hidden), bf16),
            pltpu.VMEM((2, rows, width), bf16),
            pltpu.VMEM((BLOCKS, 2) + unit, bf16),
            pltpu.VMEM((BLOCKS,) + unit, bf16),
            pltpu.VMEM((T, 2) + unit, bf16),
            pltpu.VMEM((T - 1,) + unit, bf16),
            pltpu.VMEM((BLOCKS, 8, width), f32),
            pltpu.VMEM((experts, 8, tokens), f32),
            pltpu.VMEM((experts, CAP, tokens), bf16),
            pltpu.VMEM((rows, 1), f32),
            pltpu.VMEM((rows, 128), f32),
            pltpu.VMEM((tokens, 128), f32),
            pltpu.VMEM((tokens, 1), f32),
            pltpu.VMEM((8, tokens), f32),
            pltpu.VMEM((BLOCKS - 1, 8, tokens), f32),
            pltpu.VMEM((8, tokens), f32),
            pltpu.VMEM((3, 8, tokens), f32),
            pltpu.VMEM((tokens, 1), f32),
            pltpu.VMEM(unit, bf16),
            pltpu.VMEM((8, width), f32),
            pltpu.VMEM((8, tokens), f32),
            pltpu.VMEM((width,), bf16),
            pltpu.VMEM((2, tokens), jnp.int32),
            pltpu.VMEM((2, tokens), f32),
            pltpu.VMEM(unit, bf16),
            dma((16 * T,)),
            dma((16 * T,)),
            dma((2, T + 1)),
            dma((2, T)),
            dma((len(EXTRA),)),
            dma((len(EXTRA),)),
            dma((width // TILE * BLOCKS, 8)),
            dma((width // TILE * BLOCKS, 8)),
            dma((smalls,)),
            dma((smalls,)),
            dma((2, 2)),
            dma((2,)),
            dma((6,)),
        ],
        compiler_params=pltpu.CompilerParams(
            collective_id=0, has_side_effects=True, vmem_limit_bytes=66000000
        ),
        name="fused",
    )(
        residual_stream, grad_output, norm_gain, expert_ids.T, gate_probs.T,
        w_gate[0], w_up[0], w_down[0],
    )


def solution(mesh):
    placed = (
        P("expert", ("tensor", "kv")),
        P("expert", ("tensor", "kv")),
        P(("tensor", "kv")),
        P("expert", None),
        P("expert", None),
        P("expert", ("tensor", "kv"), None),
        P("expert", ("tensor", "kv"), None),
        P("expert", ("tensor", "kv"), None),
    )
    sizes = dict(mesh.shape)
    width = D // (sizes["tensor"] * sizes["kv"])
    body = fused_shards if sizes == {"expert": 4, "tensor": 4, "kv": 2} and width % 256 == 0 else shards
    return jax.shard_map(
        body, mesh=mesh, in_specs=placed, out_specs=P("expert", ("tensor", "kv")), check_vma=False
    )
```

```python
import functools

import jax
import jax.numpy as jnp
from jax import lax
from jax.experimental import pallas as pl
from jax.experimental.pallas import tpu as pltpu
from jax.sharding import PartitionSpec as P

D = 4096
CAP = 160


epsilon = 1e-05
contract_width = (((1,), (1,)), ((), ()))
contract_hidden = (((0,), (1,)), ((), ()))
contract_slots = (((0,), (0,)), ((), ()))


def slot_matrix(ids_block, experts):
    flattened = ids_block.reshape(-1)
    onehot = (flattened[:, None] == jnp.arange(experts, dtype=jnp.int32)[None, :]).astype(jnp.int32)
    before = jnp.cumsum(onehot, axis=0) - onehot
    position = jnp.sum(before * onehot, axis=1)
    slot_index = flattened * CAP + position
    table = jnp.arange(experts * CAP, dtype=jnp.int32)
    return (slot_index[None, :] == table[:, None]).astype(jnp.bfloat16)


def shards(residual_stream, grad_output, norm_gain, expert_ids, gate_probs, w_gate, w_up, w_down):
    experts = lax.axis_size("expert")
    local_width = residual_stream.shape[1]
    tokens_here = residual_stream.shape[0]
    stream = residual_stream.astype(jnp.float32)
    squares = lax.psum(jnp.sum(stream * stream, axis=1), ("tensor", "kv"))
    inverse_rms = lax.rsqrt(squares / D + epsilon)[:, None]
    gains = norm_gain.astype(jnp.float32)
    normed = (stream * inverse_rms * gains).astype(jnp.bfloat16)
    table = slot_matrix(expert_ids, experts)
    repeated_x = jnp.repeat(normed, 2, axis=0)
    scaled = (
        jnp.repeat(grad_output.astype(jnp.float32), 2, axis=0) * gate_probs.reshape(-1, 1)
    ).astype(jnp.bfloat16)
    routed_x = jnp.dot(table, repeated_x, preferred_element_type=jnp.float32).astype(jnp.bfloat16)
    routed_grad = jnp.dot(table, scaled, preferred_element_type=jnp.float32).astype(jnp.bfloat16)
    routed_x = routed_x.reshape(experts, CAP, local_width)
    routed_grad = routed_grad.reshape(experts, CAP, local_width)
    gate_weight, up_weight, down_weight = (w_gate[0], w_up[0], w_down[0])
    pieces_x = lax.all_to_all(routed_x, "expert", split_axis=0, concat_axis=0, tiled=True)
    pieces_dy = lax.all_to_all(routed_grad, "expert", split_axis=0, concat_axis=0, tiled=True)
    full_x = lax.all_gather(pieces_x, ("tensor", "kv"), axis=2, tiled=True)
    full_dy = lax.all_gather(pieces_dy, ("tensor", "kv"), axis=2, tiled=True)
    leading = full_x.shape[0]
    items = full_x.shape[1]
    matrix_x = full_x.reshape(leading * items, D)
    matrix_dy = full_dy.reshape(leading * items, D)
    gate_value = lax.dot_general(
        matrix_x, gate_weight, contract_width, preferred_element_type=jnp.float32
    )
    up_value = lax.dot_general(
        matrix_x, up_weight, contract_width, preferred_element_type=jnp.float32
    )
    act_grad = lax.dot_general(
        matrix_dy, down_weight, contract_width, preferred_element_type=jnp.float32
    )
    sigmoid_gate = jax.nn.sigmoid(gate_value)
    activated = gate_value * sigmoid_gate
    gate_grad = (
        act_grad * up_value * sigmoid_gate * (1.0 + gate_value * (1.0 - sigmoid_gate))
    ).astype(jnp.bfloat16)
    up_grad = (act_grad * activated).astype(jnp.bfloat16)
    total = lax.dot_general(
        gate_weight, gate_grad, contract_hidden, preferred_element_type=jnp.float32
    )
    summed = lax.psum_scatter(
        total
        + lax.dot_general(up_weight, up_grad, contract_hidden, preferred_element_type=jnp.float32),
        ("tensor", "kv"),
        scatter_dimension=0,
        tiled=True,
    )
    returned = summed.T.astype(jnp.bfloat16).reshape(leading, items, local_width)
    combined = lax.all_to_all(returned, "expert", split_axis=0, concat_axis=0, tiled=True)
    gathered = lax.dot_general(
        table,
        combined.reshape(experts * CAP, local_width),
        contract_slots,
        preferred_element_type=jnp.float32,
    )
    token_grad = gathered.reshape(tokens_here, 2, local_width).sum(axis=1)
    scaled_grad = token_grad * gains
    projection = lax.psum(jnp.sum(scaled_grad * stream, axis=1), ("tensor", "kv"))[:, None]
    result = inverse_rms * scaled_grad - stream * inverse_rms**3 * projection / D
    return result.astype(jnp.bfloat16)


MESH = pl.DeviceIdType.MESH
TILE = 256
T = 4
BLOCKS = 2 * T
ORDER = [
    "0f0", "1a0", "0f1", "2a0", "1a1", "0g0", "2a1", "C000", "0h0", "D00", "C100", "0g1", "0h1", "3a0", "C001",
    "D01", "1g0", "3a1", "2g0", "e2", "e0", "C010", "2f0", "2f1", "D10", "C020", "D20", "C120", "3g0", "1x2",
    "C101", "3f0", "e1", "1g1", "C030", "3f1", "1x0", "2g1", "D30", "C130", "e3", "2h0", "C110", "1x1", "C021",
    "2h1", "D21", "C011", "3h0", "D11", "C121", "3h1", "3g1", "1x3", "C031", "D31", "C111", "C131",
]

EXTRA = [(1, 0, 1), (0, 1, 0), (0, 1, 1), (1, 1, 1)]
RETURN = [(d, s) for d in (1, 2, 3, 0) for s in (1, 0)]


def atoms_of(order):
    atoms, ahead = [], []
    for token in order:
        if token[0] == "C":
            atoms.append(dict(a=int(token[1]), i=int(token[2]), s=int(token[3]), ahead=ahead, middle=[]))
            ahead = []
        elif token[0] == "D":
            atoms[-1]["middle"], ahead = ahead, []
        else:
            ahead.append(token)
    return atoms, ahead


def pick(index, values):
    result = jnp.int32(values[0])
    for k, value in enumerate(values[1:], 1):
        if value != values[k - 1]:
            result = jnp.where(index >= k, value, result)
    return result


def fused_kernel(
    x_ref, dy_ref, gain_hbm, ids_hbm, prob_hbm, wg_ref, wu_ref, wd_ref, out_hbm,
    tok, acc, wab, wb, hid, routed, crecv, xrecv, yrecv, zrecv, gains, metas, sel, prob,
    ssq, own_sq, own_inverse, psend, precv, ptotal, pothers, factor, own_x, own_gain, own_meta, gain_ref, ids_ref, prob_ref, out_ref,
    ag_send, ag_recv, line_send, line_recv, extra_send, extra_recv, rs_send, rs_recv,
    small_send, small_recv, wasem, wbsem, lsem,
):
    e = lax.axis_index("expert")
    z = lax.axis_index("tensor")
    y = lax.axis_index("kv")
    core = e + 1 - 2 * lax.rem(e, 2)
    across = lax.rem(e + 2, 4)
    partner = z + 1 - 2 * lax.rem(z, 2)
    tokens, width = out_ref.shape
    half = tokens // 2
    hidden = wg_ref.shape[0]
    tiles = hidden // TILE
    inputs = (x_ref, dy_ref)
    low = z < 2
    layer = [z, partner, jnp.where(low, 2, 1), jnp.where(low, 3, 0)]

    def z_of(d):
        return lax.rem(z + T - d, T)

    def y_of(s):
        return y if s == 0 else 1 - y

    def fb_of(d, s):
        return z_of(d) * 2 + y_of(s)

    def seen(i, s):
        return layer[i] * 2 + y_of(s)

    def b_of(u, c):
        base = core if c else e
        return lax.rem(base + 2 * u, 4)

    def remote(src, dst, send, recv, peer):
        return pltpu.make_async_remote_copy(
            src_ref=src, dst_ref=dst, send_sem=send, recv_sem=recv,
            device_id=peer, device_id_type=MESH,
        )

    def slot(a, i, s, u, c=0):
        return tok.at[a, seen(i, s), b_of(u, c)]

    def number(a, i, s, u, c):
        return (((a * T + i) * 2 + s) * 2 + u) * 2 + c

    across_peer, side_peer, core_peer = (across, z, y), (e, z, 1 - y), (core, z, y)

    def source(a, i, s, u):
        return inputs[a] if (i, s, u) == (0, 0, 0) else slot(a, i, s, u)

    def gather_copy(a, i, s, u, c=0):
        n = number(a, i, s, u, c)
        if c:
            src, there, peer = (s, u), slot(a, i, s, u), core_peer
        elif (u and not s) or (s and u and a == 0):
            src, peer = (s, 0), across_peer
            there = slot(a, i, s, 0)
        else:
            src, peer = (0, u), side_peer
            there = slot(a, i, 0, u)
        return remote(source(a, i, *src), there, ag_send.at[n], ag_recv.at[n], peer)

    def gather_wait(a, i, s, u, c=0):
        n = number(a, i, s, u, c)
        here = slot(a, i, s, u, c)
        remote(here, here, ag_send.at[n], ag_recv.at[n], core_peer).wait_recv()

    def extra_copy(k):
        a, s, u = EXTRA[k]
        here = slot(a, 0, s, u)
        return remote(here, here, extra_send.at[k], extra_recv.at[k], (e, partner, y))

    def extra_wait(k):
        a, s, u = EXTRA[k]
        here = slot(a, 1, s, u)
        remote(here, here, extra_send.at[k], extra_recv.at[k], (e, partner, y)).wait_recv()

    def own_line(a, way):
        return remote(
            inputs[a], tok.at[a, fb_of(0, 0), e], line_send.at[a, way], line_recv.at[a, z],
            (e, z + 2 * way - 1, y),
        )

    def pass_on(a, i):
        v = layer[i]
        here = slot(a, i, 0, 0)
        return remote(
            here, here, line_send.at[a, 1 + i], line_recv.at[a, v],
            (e, jnp.where(v < z, z + 1, z - 1), y),
        )

    def passes(i):
        return jnp.where(layer[i] < z, z < T - 1, z > 0)

    sent = []

    def send(*item):
        sent.append(item)
        gather_copy(*item).start()

    def full(i):
        return i != 1

    def event(token):
        if token[0] == "e":
            extra_copy(int(token[1])).start()
            return
        i, kind, k = int(token[0]), token[1], int(token[2])
        if kind == "a":
            pass_on(k, i).wait_recv()

            @pl.when(passes(i))
            def _():
                pass_on(k, i).start()

            if full(i):
                send(k, i, *((1, 0) if k == 0 else (0, 1)))
                send(k, i, *((0, 1) if k == 0 else (1, 0)))
            else:
                send(k, i, *((0, 1) if k == 0 else (1, 0)))
            send(k, i, 0, 0, 1)
            return
        if kind == "x":
            extra_wait(k)
            send(EXTRA[k][0], i, *EXTRA[k][1:], 1)
            return
        first = (1, 0) if k == 0 else (0, 1)
        s, u = {"f": first, "g": first[::-1], "h": (1, 1)}[kind]
        gather_wait(k, i, s, u)
        if kind == "f":
            send(k, i, 1, 1)
        send(k, i, s, u, 1)

    atoms, rest = atoms_of(ORDER)
    wide = [atom for atom in atoms if atom["a"] == 0]
    tall = [atom for atom in atoms if atom["a"] == 1]

    def fb_at(index, group):
        return select(index, [layer[atom["i"]] * 2 + y_of(atom["s"]) for atom in group])

    def select(index, values):
        result = values[0]
        for k, value in enumerate(values[1:], 1):
            result = jnp.where(index >= k, value, result)
        return result

    return_fb = [fb_of(*item) for item in RETURN]

    def columns_of(fb):
        return pl.ds(pl.multiple_of(fb * width, width), width)

    def wide_copies(index, place):
        columns = columns_of(place)
        at = lax.rem(index, 2)
        return [
            pltpu.make_async_copy(ref.at[:, columns], wab.at[at, k], wasem.at[at, k])
            for k, ref in enumerate((wg_ref, wu_ref))
        ]

    def tall_copy(index, place):
        at = lax.rem(index, 2)
        return pltpu.make_async_copy(wd_ref.at[:, columns_of(place)], wb.at[at], wbsem.at[at])

    local = [
        pltpu.make_async_copy(x_ref, tok.at[0, fb_of(0, 0), e], lsem.at[0]),
        pltpu.make_async_copy(dy_ref, tok.at[1, fb_of(0, 0), e], lsem.at[1]),
    ]
    tables = [
        pltpu.make_async_copy(gain_hbm, gain_ref, lsem.at[3]),
        pltpu.make_async_copy(ids_hbm, ids_ref, lsem.at[4]),
        pltpu.make_async_copy(prob_hbm, prob_ref, lsem.at[5]),
    ]
    peers = [(e, lax.rem(z + d, T), y_of(s)) for d in range(T) for s in (0, 1) if d or s]
    sources = [fb_of(d, s) for d in range(T) for s in (0, 1) if d or s]
    others = [(lax.rem(e + k, 4), z, y) for k in (1, 2, 3)]
    barrier = pltpu.get_barrier_semaphore()
    for peer in peers + others:
        pl.semaphore_signal(barrier, inc=1, device_id=peer, device_id_type=MESH)
    for copy in tables + local:
        copy.start()
    pl.semaphore_wait(barrier, len(peers) + len(others))

    for item in ((0, 0, 1, 0), (1, 0, 0, 1), (0, 0, 0, 1), (1, 0, 1, 0)):
        send(*item)
    for a in (0, 1):
        for way in (0, 1):
            @pl.when(z < T - 1 if way else z > 0)
            def _():
                own_line(a, way).start()
    for a in (0, 1):
        send(a, 0, 0, 0, 1)
    for copy in wide_copies(0, fb_at(0, wide)) + [tall_copy(0, fb_at(0, tall))]:
        copy.start()

    for copy in tables:
        copy.wait()
    number_of = lax.broadcasted_iota(jnp.int32, (8, tokens), 0)
    named_by = jnp.where(number_of < 4, number_of, number_of - 4)
    first = jnp.broadcast_to(ids_ref[0:1, :], (8, tokens)) == named_by
    second = jnp.broadcast_to(ids_ref[1:2, :], (8, tokens)) == named_by
    named = jnp.where(first, 1.0, 0.0) + jnp.where(second, 1.0, 0.0)
    later = (
        lax.broadcasted_iota(jnp.int32, (tokens, tokens), 0)
        < lax.broadcasted_iota(jnp.int32, (tokens, tokens), 1)
    )
    before = jnp.dot(
        named.astype(jnp.bfloat16), jnp.where(later, 1.0, 0.0).astype(jnp.bfloat16),
        preferred_element_type=jnp.float32,
    )
    weight = jnp.where(first, jnp.broadcast_to(prob_ref[0:1, :], (8, tokens)), 0.0) + jnp.where(
        second, jnp.broadcast_to(prob_ref[1:2, :], (8, tokens)), 0.0
    )
    own_meta[...] = jnp.where(number_of < 4, jnp.where(named > 0.0, before, -1.0), weight)
    metas[e] = own_meta[...]
    own_gain[...] = jnp.broadcast_to(gain_ref[...].astype(jnp.float32)[None, :], own_gain.shape)
    gains[fb_of(0, 0)] = own_gain[...]

    small = []
    for k, peer in enumerate(others):
        copy = remote(own_meta, metas.at[e], small_send.at[k], small_recv.at[k], peer)
        copy.start()
        there = metas.at[lax.rem(e + 3 - k, 4)]
        small.append((copy, remote(there, there, small_send.at[k], small_recv.at[k], peer)))
    for k, peer in enumerate(peers):
        n = 3 + k
        copy = remote(own_gain, gains.at[fb_of(0, 0)], small_send.at[n], small_recv.at[n], peer)
        copy.start()
        there = gains.at[sources[k]]
        small.append((copy, remote(there, there, small_send.at[n], small_recv.at[n], peer)))

    own_sq[...] = jnp.zeros_like(own_sq)
    ssq[...] = jnp.zeros_like(ssq)

    def clear(n, carry):
        for k in range(3):
            acc[k, n] = jnp.zeros(acc.shape[2:], jnp.float32)
        return carry

    lax.fori_loop(0, tiles, clear, 0)
    for copy, arrival in small[:3]:
        arrival.wait_recv()
    for b in range(4):
        slots = metas[b, pl.ds(e, 1), :]
        probs = metas[b, pl.ds(4 + e, 1), :]
        index = lax.broadcasted_iota(jnp.int32, (CAP, slots.shape[1]), 0).astype(jnp.float32)
        chosen = jnp.where(index == slots, 1.0, 0.0)
        sel[b] = chosen.astype(jnp.bfloat16)
        prob[pl.ds(b * CAP, CAP), :] = jnp.sum(chosen * probs, axis=1, keepdims=True)
    for copy, arrival in small[3:]:
        arrival.wait_recv()
    for copy in local:
        copy.wait()

    def by_lane(value):
        square = value * value
        lanes = [square[:, k : k + 128] for k in range(0, width, 128)]
        return sum(lanes[1:], lanes[0])

    def accumulate(k, source, weights):
        for n in range(tiles):
            acc[k, n] += lax.dot_general(
                source[...], weights[n * TILE : (n + 1) * TILE, :], contract_width,
                preferred_element_type=jnp.float32,
            )

    def dispatch(index, low, high, run, used):
        if not any(k in used for k in range(low, high)):
            return
        if high - low == 1:
            run(low)
            return
        middle = (low + high) // 2
        for cond, first, last in ((index < middle, low, middle), (index >= middle, middle, high)):
            if any(k in used for k in range(first, last)):
                @pl.when(cond)
                def _():
                    dispatch(index, first, last, run, used)

    def gather_step(j, carry):
        def before_atom(k):
            for token in atoms[k]["ahead"]:
                event(token)
            for u in (0, 1):
                gather_wait(atoms[k]["a"], atoms[k]["i"], atoms[k]["s"], u, 1)

        def amid_atom(k):
            for token in atoms[k]["middle"]:
                event(token)

        dispatch(j, 0, len(atoms), before_atom, range(len(atoms)))

        kinds = [atom["a"] for atom in atoms]
        ranks = [sum(kinds[:k]) for k in range(len(atoms))]
        kind = pick(j, kinds)
        tall_rank = pick(j, ranks)
        wide_rank = j - tall_rank

        @pl.when(kind == 0)
        def _():
            following = jnp.where(
                wide_rank < BLOCKS - 1, fb_at(wide_rank + 1, wide), return_fb[0]
            )
            for copy in wide_copies(wide_rank + 1, following):
                copy.start()
            fb = fb_at(wide_rank, wide)
            gain_row = gains[fb, 0:1, :]
            mine = tok[0, fb, e].astype(jnp.float32)
            own_sq[...] += by_lane(mine)
            for b in range(4):
                rows = pl.ds(b * CAP, CAP)
                picked = jnp.dot(sel[b], tok[0, fb, b], preferred_element_type=jnp.float32)
                ssq[rows, :] += by_lane(picked)
                routed[0, rows, :] = (picked * gain_row).astype(jnp.bfloat16)
            for copy in wide_copies(wide_rank, fb):
                copy.wait()
            at = lax.rem(wide_rank, 2)
            accumulate(0, routed.at[0], wab.at[at, 0])
            dispatch(j, 0, len(atoms), amid_atom, [k for k, atom in enumerate(atoms) if atom["middle"]])
            accumulate(1, routed.at[0], wab.at[at, 1])

        @pl.when(kind == 1)
        def _():
            @pl.when(tall_rank < BLOCKS - 1)
            def _():
                tall_copy(tall_rank + 1, fb_at(tall_rank + 1, tall)).start()

            fb = fb_at(tall_rank, tall)
            for b in range(4):
                rows = pl.ds(b * CAP, CAP)
                picked = jnp.dot(sel[b], tok[1, fb, b], preferred_element_type=jnp.float32)
                routed[1, rows, :] = (picked * prob[rows, :]).astype(jnp.bfloat16)
            tall_copy(tall_rank, fb).wait()
            accumulate(2, routed.at[1], wb.at[lax.rem(tall_rank, 2)])

        return carry

    lax.fori_loop(0, len(atoms), gather_step, 0)
    for token in rest:
        event(token)
    reload = pltpu.make_async_copy(x_ref, own_x, lsem.at[2])
    reload.start()
    for item in sent:
        gather_copy(*item).wait_send()
    for a in (0, 1):
        for way in (0, 1):
            @pl.when(z < T - 1 if way else z > 0)
            def _():
                own_line(a, way).wait_send()
        for i in range(1, T):
            @pl.when(passes(i))
            def _():
                pass_on(a, i).wait_send()
    for k in range(len(EXTRA)):
        extra_copy(k).wait_send()
    for copy, arrival in small:
        copy.wait_send()

    inverse = lax.rsqrt(jnp.sum(ssq[...], axis=1, keepdims=True) / D + epsilon)

    def activate(n, start):
        columns = pl.ds(pl.multiple_of(n * TILE, TILE), TILE)
        gate_sum, up_sum, act_grad = acc[0, n], acc[1, n], acc[2, n]
        gate_value = gate_sum * inverse
        up_value = up_sum * inverse
        sigmoid_gate = jax.nn.sigmoid(gate_value)
        gate_grad = (
            act_grad * up_value * sigmoid_gate * (1.0 + gate_value * (1.0 - sigmoid_gate))
        ).astype(jnp.bfloat16)
        up_grad = (act_grad * gate_value * sigmoid_gate).astype(jnp.bfloat16)
        hid[0, :, columns] = gate_grad
        hid[1, :, columns] = up_grad
        term = gate_grad.astype(jnp.float32) * gate_sum + up_grad.astype(jnp.float32) * up_sum
        acc[2, 0] = term if start else acc[2, 0] + term

    def activate_more(n, carry):
        activate(n, False)
        return carry

    activate(0, True)
    lax.fori_loop(1, tiles, activate_more, 0)

    def share_copies():
        return [
            remote(psend, precv.at[k], small_send.at[10 + k], small_recv.at[10 + k], peer)
            for k, peer in enumerate(peers)
        ]

    def total_copies():
        return [
            remote(ptotal, pothers.at[k], small_send.at[17 + k], small_recv.at[17 + k], peer)
            for k, peer in enumerate(others)
        ]

    def share_projection():
        pairs = jnp.sum(acc[2, 0], axis=1, keepdims=True)
        for b in range(4):
            of_block = sel[b].astype(jnp.float32) * pairs[b * CAP : (b + 1) * CAP]
            psend[b : b + 1, :] = jnp.sum(of_block, axis=0, keepdims=True)
        psend[4:8, :] = jnp.zeros((4, tokens), jnp.float32)
        for copy in share_copies():
            copy.start()

    def total_projection():
        for copy in share_copies():
            copy.wait_recv()
        row = psend[...]
        for k in range(len(peers)):
            row = row + precv[k]
        ptotal[...] = row
        for copy in total_copies():
            copy.start()

    def finish_projection():
        for copy in total_copies():
            copy.wait_recv()
        row = ptotal[pl.ds(e, 1), :]
        for k in range(len(others)):
            row = row + pothers[k, pl.ds(e, 1), :]
        projection = jnp.broadcast_to(row, (128, tokens)).T[:, 0:1]
        inverse = lax.rsqrt(jnp.sum(own_sq[...], axis=1, keepdims=True) / D + epsilon)
        own_inverse[...] = inverse
        factor[...] = inverse * inverse * inverse * projection / D

    upper, lower, everything = pl.ds(0, half), pl.ds(half, half), pl.ds(0, tokens)
    halves = width // TILE

    def place(m):
        i, n = m // halves, m % halves
        return i, *RETURN[i], pl.ds(n * TILE, TILE)

    def core_copy(m, u):
        i, n = m // halves, m % halves
        columns = pl.ds(pl.multiple_of(n * TILE, TILE), TILE)
        return remote(
            tok.at[0, i, lax.rem(core + 2 * u, 4), :, columns], crecv.at[i, u, :, columns],
            rs_send.at[m, u], rs_recv.at[m, u], core_peer,
        )

    def across_copy(m, h):
        i, d, s, columns = place(m)
        rows = lower if h else upper
        return remote(
            tok.at[1, i, 0, rows, columns], xrecv.at[i, rows, columns],
            rs_send.at[m, 2 + h], rs_recv.at[m, 2 + h], across_peer,
        )

    def side_copy(m, u, h):
        i, d, s, columns = place(m)
        rows = lower if h else upper
        n = 4 + (u if h else 2)
        return remote(
            tok.at[1, i, 0 if u else 1, rows, columns], yrecv.at[d, u, rows, columns],
            rs_send.at[m, n], rs_recv.at[m, n], side_peer,
        )

    def line_copy(m):
        i, d, s, columns = place(m)
        return remote(
            tok.at[1, i, 2, :, columns], zrecv.at[d - 1, :, columns],
            rs_send.at[m, 7], rs_recv.at[m, 7], (e, z_of(d), y),
        )

    def total(rows, columns, *parts):
        value = parts[0][rows, columns].astype(jnp.float32)
        for part in parts[1:]:
            value = value + part[rows, columns].astype(jnp.float32)
        return value

    def first_stage(m):
        i, d, s, columns = place(m)
        core_copy(m, 1).wait_recv()
        far = (tok.at[0, i, across], crecv.at[i, 1])
        if s:
            tok[1, i, 0, :, columns] = total(everything, columns, *far).astype(jnp.bfloat16)
            across_copy(m, 0).start()
            side_copy(m, 1, 1).start()
            core_copy(m, 0).wait_recv()
            tok[1, i, 1, lower, columns] = total(
                lower, columns, tok.at[0, i, e], crecv.at[i, 0]
            ).astype(jnp.bfloat16)
            side_copy(m, 0, 1).start()
        else:
            tok[1, i, 0, upper, columns] = total(upper, columns, *far).astype(jnp.bfloat16)
            across_copy(m, 0).start()

    def second_stage(m):
        i, d, s, columns = place(m)
        if s:
            across_copy(m, 0).wait_recv()
            tok[1, i, 1, upper, columns] = total(
                upper, columns, tok.at[0, i, e], crecv.at[i, 0], xrecv.at[i]
            ).astype(jnp.bfloat16)
            side_copy(m, 0, 0).start()
        else:
            side_copy(m - halves, 1, 1).wait_recv()
            tok[1, i, 0, lower, columns] = total(
                lower, columns, tok.at[0, i, across], crecv.at[i, 1], yrecv.at[d, 1]
            ).astype(jnp.bfloat16)
            across_copy(m, 1).start()

    def third_stage(m):
        i, d, s, columns = place(m)
        core_copy(m, 0).wait_recv()
        across_copy(m, 0).wait_recv()
        side_copy(m - halves, 0, 1).wait_recv()
        side_copy(m - halves, 0, 0).wait_recv()
        across_copy(m, 1).wait_recv()
        value = total(everything, columns, tok.at[0, i, e], crecv.at[i, 0], xrecv.at[i], yrecv.at[d, 0])
        if d:
            tok[1, i, 2, :, columns] = value.astype(jnp.bfloat16)
            line_copy(m).start()
        else:
            acc[0, m % halves, everything, :] = value

    stages = {}
    for m in range(halves * BLOCKS):
        plan = [(1, first_stage), (4, second_stage)] if place(m)[2] else (
            [(1, first_stage), (2, second_stage), (5, third_stage)]
        )
        for when, stage in plan:
            stages.setdefault(m + 1 + when, []).append((stage, m))

    projection_steps = {2: share_projection, 9: total_projection, 15: finish_projection}

    def run_stages(k):
        for stage, m in stages.get(k, []):
            stage(m)
        if k in projection_steps:
            projection_steps[k]()

    def produce(h, carry):

        dispatch(h, 0, halves * BLOCKS, run_stages, [*stages, *projection_steps])

        i, n = h // halves, lax.rem(h, halves)

        @pl.when(jnp.logical_and(n == 0, i < BLOCKS - 1))
        def _():
            for copy in wide_copies(i + 1, select(i + 1, return_fb)):
                copy.start()

        @pl.when(n == 0)
        def _():
            for copy in wide_copies(i, select(i, return_fb)):
                copy.wait()

        at = lax.rem(i, 2)
        columns = pl.ds(pl.multiple_of(n * TILE, TILE), TILE)
        rounded = (
            jnp.dot(hid[0], wab[at, 0, :, columns], preferred_element_type=jnp.float32)
            + jnp.dot(hid[1], wab[at, 1, :, columns], preferred_element_type=jnp.float32)
        ).astype(jnp.bfloat16)
        for b in range(4):
            tok[0, i, b, :, columns] = lax.dot_general(
                sel[b], rounded[b * CAP : (b + 1) * CAP], contract_slots,
                preferred_element_type=jnp.float32,
            ).astype(jnp.bfloat16)

        core_copy(h, 1).start()
        core_copy(h, 0).start()
        return carry

    lax.fori_loop(0, halves * BLOCKS, produce, 0)
    for key in sorted({*stages, *projection_steps}):
        if key >= halves * BLOCKS:
            run_stages(key)
    reload.wait()
    for n in range(halves):
        columns = pl.ds(n * TILE, TILE)
        value = acc[0, n, everything, :]
        for i, (d, s) in enumerate(RETURN):
            if d and not s:
                line_copy(halves * i + n).wait_recv()
                value = value + zrecv[d - 1, :, columns].astype(jnp.float32)
        scaled = value * gains[fb_of(0, 0), 0:1, columns]
        stream = own_x[:, columns].astype(jnp.float32)
        out_ref[:, columns] = (own_inverse[...] * scaled - stream * factor[...]).astype(out_ref.dtype)
    written = pltpu.make_async_copy(out_ref, out_hbm, lsem.at[2])
    written.start()
    for copy in share_copies() + total_copies():
        copy.wait_send()
    for m in range(halves * BLOCKS):
        i, d, s, columns = place(m)
        core_copy(m, 0).wait_send()
        core_copy(m, 1).wait_send()
        across_copy(m, 0).wait_send()
        if s:
            side_copy(m, 1, 1).wait_send()
            side_copy(m, 0, 1).wait_send()
            side_copy(m, 0, 0).wait_send()
        else:
            across_copy(m, 1).wait_send()
            if d:
                line_copy(m).wait_send()
    written.wait()


def fused_shards(residual_stream, grad_output, norm_gain, expert_ids, gate_probs, w_gate, w_up, w_down):
    experts = lax.axis_size("expert")
    tokens, width = residual_stream.shape
    hidden = w_gate.shape[1]
    bf16, f32 = jnp.bfloat16, jnp.float32
    rows = experts * CAP
    hbm = pl.BlockSpec(memory_space=pl.ANY)
    dma = pltpu.SemaphoreType.DMA
    unit = (tokens, width)
    smalls = 3 + 2 * (BLOCKS - 1) + 3
    return pl.pallas_call(
        fused_kernel,
        out_shape=jax.ShapeDtypeStruct(unit, bf16),
        in_specs=[hbm] * 8,
        out_specs=hbm,
        scratch_shapes=[
            pltpu.VMEM((2, BLOCKS, experts) + unit, bf16),
            pltpu.VMEM((3, hidden // TILE, rows, TILE), f32),
            pltpu.VMEM((2, 2, hidden, width), bf16),
            pltpu.VMEM((2, hidden, width), bf16),
            pltpu.VMEM((2, rows, hidden), bf16),
            pltpu.VMEM((2, rows, width), bf16),
            pltpu.VMEM((BLOCKS, 2) + unit, bf16),
            pltpu.VMEM((BLOCKS,) + unit, bf16),
            pltpu.VMEM((T, 2) + unit, bf16),
            pltpu.VMEM((T - 1,) + unit, bf16),
            pltpu.VMEM((BLOCKS, 8, width), f32),
            pltpu.VMEM((experts, 8, tokens), f32),
            pltpu.VMEM((experts, CAP, tokens), bf16),
            pltpu.VMEM((rows, 1), f32),
            pltpu.VMEM((rows, 128), f32),
            pltpu.VMEM((tokens, 128), f32),
            pltpu.VMEM((tokens, 1), f32),
            pltpu.VMEM((8, tokens), f32),
            pltpu.VMEM((BLOCKS - 1, 8, tokens), f32),
            pltpu.VMEM((8, tokens), f32),
            pltpu.VMEM((3, 8, tokens), f32),
            pltpu.VMEM((tokens, 1), f32),
            pltpu.VMEM(unit, bf16),
            pltpu.VMEM((8, width), f32),
            pltpu.VMEM((8, tokens), f32),
            pltpu.VMEM((width,), bf16),
            pltpu.VMEM((2, tokens), jnp.int32),
            pltpu.VMEM((2, tokens), f32),
            pltpu.VMEM(unit, bf16),
            dma((16 * T,)),
            dma((16 * T,)),
            dma((2, T + 1)),
            dma((2, T)),
            dma((len(EXTRA),)),
            dma((len(EXTRA),)),
            dma((width // TILE * BLOCKS, 8)),
            dma((width // TILE * BLOCKS, 8)),
            dma((smalls,)),
            dma((smalls,)),
            dma((2, 2)),
            dma((2,)),
            dma((6,)),
        ],
        compiler_params=pltpu.CompilerParams(
            collective_id=0, has_side_effects=True, vmem_limit_bytes=66000000
        ),
        name="fused",
    )(
        residual_stream, grad_output, norm_gain, expert_ids.T, gate_probs.T,
        w_gate[0], w_up[0], w_down[0],
    )


def solution(mesh):
    placed = (
        P("expert", ("tensor", "kv")),
        P("expert", ("tensor", "kv")),
        P(("tensor", "kv")),
        P("expert", None),
        P("expert", None),
        P("expert", ("tensor", "kv"), None),
        P("expert", ("tensor", "kv"), None),
        P("expert", ("tensor", "kv"), None),
    )
    sizes = dict(mesh.shape)
    width = D // (sizes["tensor"] * sizes["kv"])
    body = fused_shards if sizes == {"expert": 4, "tensor": 4, "kv": 2} and width % 256 == 0 else shards
    return jax.shard_map(
        body, mesh=mesh, in_specs=placed, out_specs=P("expert", ("tensor", "kv")), check_vma=False
    )
```
